32 devices in a mesh: dp: 2 (over x), ctx: 16 (over z, y, core).
Axes of the slice: x: 2, y: 2, z: 4, core: 2. Of those that a mesh axis runs over, the one named last changes fastest.
Arguments:
- layer_in: bfloat16 [4, 1024, 1600], P('dp', 'ctx'), may hold values from -6 to 6
- out_grad: bfloat16 [4, 1024, 1600], P('dp', 'ctx'), may hold values from -6 to 6
- block_order: int32 [4, 32], P('dp'), may hold values from 0 to 31, as said below
- ln1_gain: float32 [1600], replicated, may hold values from 0.5 to 1.5
- ln1_bias: float32 [1600], replicated, may hold values from -3 to 3
- w_qkv: bfloat16 [1600, 4800], P(None, 'dp'), may hold values from -5 to 5
- qv_bias: float32 [2, 1600], replicated, may hold values from -3 to 3
- w_out: bfloat16 [1600, 1600], P(None, 'dp'), may hold values from -1.5 to 1.5
- out_bias: float32 [1600], replicated, may hold values from -3 to 3
- ln2_gain: float32 [1600], replicated, may hold values from 0.5 to 1.5
- ln2_bias: float32 [1600], replicated, may hold values from -3 to 3
- w_up: bfloat16 [1600, 6400], P(None, 'dp'), may hold values from -0.15625 to 0.15625
- up_bias: float32 [6400], replicated, may hold values from -3 to 3
- w_down: bfloat16 [6400, 1600], P(None, 'dp'), may hold values from -0.078125 to 0.078125
- down_bias: float32 [1600], replicated, may hold values from -3 to 3
Outputs:
- layer_out: bfloat16 [4, 1024, 1600], P('dp', 'ctx')
- input_grad: bfloat16 [4, 1024, 1600], P('dp', 'ctx')
- ln1_gain_grad: float32 [1600], replicated
- ln1_bias_grad: float32 [1600], replicated
- w_qkv_grad: float32 [1600, 4800], P('dp', 'ctx')
- qv_bias_grad: float32 [2, 1600], replicated
- w_out_grad: float32 [1600, 1600], P('ctx', 'dp')
- out_bias_grad: float32 [1600], replicated
- ln2_gain_grad: float32 [1600], replicated
- ln2_bias_grad: float32 [1600], replicated
- w_up_grad: float32 [1600, 6400], P('dp', 'ctx')
- up_bias_grad: float32 [6400], replicated
- w_down_grad: float32 [6400, 1600], P('ctx', 'dp')
- down_bias_grad: float32 [1600], replicated
The draws below stay inside these ranges and needn't reach their ends.
Inputs may be any that keep to these rules, and one draw needn't show every extreme that they name: `block_order`: each row is a permutation of the half-blocks. Slots 2c and 2c + 1 together hold one unit p (the same p for no two c): in a row of the contiguous form half-blocks 2p and 2p + 1, in a row of the paired form half-blocks p and 31 - p. Each sequence has one form.
All inputs are finite; a program needn't handle non-finite values.
Results may differ from the reference program's by a relative error of at most 0.015.
The reference program's roundings to bfloat16 on the way count: a program that leaves them out, or rounds other values in their place, can miss the bound.
Values may be sent and summed in bfloat16 or wider, within the bound.
No kernel may reach another device: no remote copies, remote signals or barrier semaphores. Data moves between devices by JAX's collectives and lax.ppermute only.
A program may use at most 576 MiB of HBM per device.

```python
import math
import jax
import jax.numpy as jnp
from jax import lax

D = 1600
HEADS = 25
HEAD_DIM = 64
FF = 6400
LEN = 1024
SLOTS = 32
SEQS = 4


def order_one(key):
    unit_count = SLOTS // 2
    perm_key = jax.random.fold_in(key, 11)
    form_key = jax.random.fold_in(key, 13)
    unit_perm = jax.random.permutation(perm_key, unit_count).astype(jnp.int32)
    form = jax.random.randint(form_key, (), 0, 2, dtype=jnp.int32)
    slot_ids = jnp.arange(SLOTS, dtype=jnp.int32)
    pair_ids = slot_ids // 2
    lower = slot_ids % 2
    unit_table = pair_ids[:, None] == jnp.arange(unit_count, dtype=jnp.int32)[None, :]
    units = jnp.sum(jnp.where(unit_table, unit_perm[None, :], 0), axis=1).astype(jnp.int32)
    contiguous = 2 * units + lower
    paired = jnp.where(lower == 0, units, SLOTS - 1 - units)
    return jnp.where(form == 1, paired, contiguous).astype(jnp.int32)


def draw_block_order(key, part):
    seq_keys = jax.random.split(key, SEQS)
    return jax.vmap(order_one)(seq_keys).astype(jnp.int32)


def draw_w_qkv(key, part):
    normal_draw = jnp.clip(jax.random.normal(key, (D, 3 * D), jnp.float32), -6.0, 6.0) * D ** (-0.5)
    return jnp.clip(normal_draw, -5.0, 5.0).astype(jnp.bfloat16)


def steps_of(own_key, dims, cuts, least, largest):
    def one(dim, blocks):
        steps = jax.random.uniform(jax.random.fold_in(jax.random.fold_in(own_key, 6), dim), (blocks,), jnp.float32, least / len(cuts), largest / len(cuts))
        return jnp.repeat(jnp.exp(steps), dims[dim] // blocks).reshape((-1,) + (1,) * (len(dims) - dim - 1))

    factor_of = one(*cuts[0])
    for cut in cuts[1:]:
        factor_of = factor_of * one(*cut)
    return factor_of


def scatter_about(rng, dims, deviation, most, pieces=(), held_as=jnp.bfloat16):
    result = jax.random.normal(rng, dims, jnp.float32) * deviation
    if len(pieces) > 0:
        result = steps_of(rng, dims, pieces, -0.22, 0.18) * result
    return jnp.clip(result, min=-most, max=most).astype(held_as)


def setup_inputs(seed: int = 0) -> dict:
    splits = jax.random.split(jax.random.key(seed), 16)
    return {
        "layer_in": scatter_about(splits[0], (SEQS, LEN, D), 1.0, 6.0, ((0, 2), (1, 16))),
        "out_grad": scatter_about(splits[1], (SEQS, LEN, D), 1.0, 6.0, ((0, 2), (1, 16))),
        "block_order": draw_block_order(jax.random.fold_in(splits[15], 71), 0),
        "ln1_gain": jnp.clip(1.0 + 0.1 * jax.random.normal(splits[3], (D,), jnp.float32), 0.5, 1.5),
        "ln1_bias": scatter_about(splits[4], (D,), 0.5, 3.0, (), jnp.float32),
        "w_qkv": draw_w_qkv(jax.random.fold_in(splits[15], 71), 0),
        "qv_bias": scatter_about(splits[6], (2, D), 0.5, 3.0, (), jnp.float32),
        "w_out": scatter_about(splits[7], (D, D), 16 ** -0.5, 1.5, ((1, 2),)),
        "out_bias": scatter_about(splits[8], (D,), 0.5, 3.0, (), jnp.float32),
        "ln2_gain": jnp.clip(1.0 + 0.1 * jax.random.normal(splits[9], (D,), jnp.float32), 0.5, 1.5),
        "ln2_bias": scatter_about(splits[10], (D,), 0.5, 3.0, (), jnp.float32),
        "w_up": scatter_about(splits[11], (D, FF), D ** -0.5, 0.15625, ((1, 2),)),
        "up_bias": scatter_about(splits[12], (FF,), 0.5, 3.0, (), jnp.float32),
        "w_down": scatter_about(splits[13], (FF, D), FF ** -0.5, 0.078125, ((1, 2),)),
        "down_bias": scatter_about(splits[14], (D,), 0.5, 3.0, (), jnp.float32),
    }


EPS = 1e-05
GELU_C = 0.7978845608028654
NEG_FILL = -1e+30

def normalize(row_data):
    centre = lax.optimization_barrier(jnp.mean(row_data, axis=-1, keepdims=True))
    shifted = row_data - centre
    inverse = lax.rsqrt(lax.optimization_barrier(jnp.mean(shifted * shifted, axis=-1, keepdims=True)) + EPS)
    return (shifted * inverse, inverse)

def norm_back(grad_hat, normed, inverse):
    first_mean = lax.optimization_barrier(jnp.mean(grad_hat, axis=-1, keepdims=True))
    second = lax.optimization_barrier(jnp.mean(grad_hat * normed, axis=-1, keepdims=True))
    return inverse * (grad_hat - first_mean - normed * second)

def gelu_parts(values):
    cubic_term = 0.044715 * values * values * values
    tangent = jnp.tanh(GELU_C * (values + cubic_term))
    output = 0.5 * values * (1.0 + tangent)
    gelu_slope = 0.5 * (1.0 + tangent) + 0.5 * values * (1.0 - tangent * tangent) * GELU_C * (1.0 + 3.0 * 0.044715 * values * values)
    return (output, gelu_slope)

def attend_forward(query_heads, key_heads, value_heads):
    length = query_heads.shape[0]
    block_rows = math.gcd(length, 256)
    score_scale = 1.0 / math.sqrt(HEAD_DIM)
    key_wide = key_heads.astype(jnp.float32)
    value_wide = value_heads.astype(jnp.float32)
    key_ids = jnp.arange(length, dtype=jnp.int32)

    def visit_block(accumulated, block_index):
        first_row = block_index * block_rows
        query_block = lax.dynamic_slice_in_dim(query_heads, first_row, block_rows, 0).astype(jnp.float32)
        query_ids = first_row + jnp.arange(block_rows, dtype=jnp.int32)
        scores = jnp.einsum('qhd,khd->hqk', query_block, key_wide) * score_scale
        visible = (key_ids[None, :] <= query_ids[:, None])[None]
        row_max = lax.optimization_barrier(jnp.max(jnp.where(visible, scores, NEG_FILL), axis=-1))
        weights = jnp.where(visible, jnp.exp(scores - row_max[:, :, None]), 0.0)
        row_sum = lax.optimization_barrier(jnp.sum(weights, axis=-1))
        summed = jnp.einsum('hqk,khd->qhd', weights, value_wide, precision=lax.Precision.HIGHEST)
        output = (summed / row_sum.T[:, :, None]).astype(jnp.bfloat16)
        return (accumulated, (output, (row_max + jnp.log(row_sum)).T))
    unused, (outputs, log_rows) = lax.scan(visit_block, jnp.zeros((), jnp.int32), jnp.arange(length // block_rows, dtype=jnp.int32))
    return (outputs.reshape(length, HEADS, HEAD_DIM), log_rows.reshape(length, HEADS))

def attend_backward(query_heads, key_heads, value_heads, grad_heads, out_heads, log_rows):
    length = query_heads.shape[0]
    block_rows = math.gcd(length, 256)
    score_scale = 1.0 / math.sqrt(HEAD_DIM)
    key_wide = key_heads.astype(jnp.float32)
    value_wide = value_heads.astype(jnp.float32)
    key_ids = jnp.arange(length, dtype=jnp.int32)
    deltas = lax.optimization_barrier(jnp.sum(grad_heads.astype(jnp.float32) * out_heads.astype(jnp.float32), axis=-1))

    def visit_block(accumulated, block_index):
        grad_keys, grad_values = accumulated
        first_row = block_index * block_rows
        query_block = lax.dynamic_slice_in_dim(query_heads, first_row, block_rows, 0).astype(jnp.float32)
        grad_block = lax.dynamic_slice_in_dim(grad_heads, first_row, block_rows, 0).astype(jnp.float32)
        log_block = lax.dynamic_slice_in_dim(log_rows, first_row, block_rows, 0)
        delta_block = lax.dynamic_slice_in_dim(deltas, first_row, block_rows, 0)
        query_ids = first_row + jnp.arange(block_rows, dtype=jnp.int32)
        scores = jnp.einsum('qhd,khd->hqk', query_block, key_wide) * score_scale
        visible = (key_ids[None, :] <= query_ids[:, None])[None]
        probabilities = jnp.where(visible, jnp.exp(scores - log_block.T[:, :, None]), 0.0)
        rounded = lax.optimization_barrier(probabilities.astype(jnp.bfloat16)).astype(jnp.float32)
        grad_values = grad_values + jnp.einsum('hqk,qhd->khd', rounded, grad_block)
        grad_probs = jnp.einsum('qhd,khd->hqk', grad_block, value_wide)
        grad_scores = probabilities * (grad_probs - delta_block.T[:, :, None]) * score_scale
        grad_scores = lax.optimization_barrier(grad_scores.astype(jnp.bfloat16)).astype(jnp.float32)
        grad_query = jnp.einsum('hqk,khd->qhd', grad_scores, key_wide)
        grad_keys = grad_keys + jnp.einsum('hqk,qhd->khd', grad_scores, query_block)
        return ((grad_keys, grad_values), grad_query)
    zero_heads = jnp.zeros((length, HEADS, HEAD_DIM), jnp.float32)
    (grad_keys, grad_values), grad_queries = lax.scan(visit_block, (zero_heads, zero_heads), jnp.arange(length // block_rows, dtype=jnp.int32))
    return (grad_queries.reshape(length, HEADS, HEAD_DIM), grad_keys, grad_values)

def one_sequence(stream_rows, grad_rows, parameters):
    ln1_gain, ln1_bias, w_qkv, qv_bias, w_out, out_bias, ln2_gain, ln2_bias, w_up, up_bias, w_down, down_bias = parameters
    length = stream_rows.shape[0]
    stream = stream_rows.astype(jnp.float32)
    normed_one, inverse_one = normalize(stream)
    hidden_one = (normed_one * ln1_gain + ln1_bias).astype(jnp.bfloat16)
    projected = jnp.dot(hidden_one, w_qkv, preferred_element_type=jnp.float32)
    queries = (projected[:, :D] + qv_bias[0]).astype(jnp.bfloat16)
    keys_all = projected[:, D:2 * D].astype(jnp.bfloat16)
    values_all = (projected[:, 2 * D:] + qv_bias[1]).astype(jnp.bfloat16)
    query_heads = queries.reshape(length, HEADS, HEAD_DIM)
    key_heads = keys_all.reshape(length, HEADS, HEAD_DIM)
    value_heads = values_all.reshape(length, HEADS, HEAD_DIM)
    out_heads, log_rows = attend_forward(query_heads, key_heads, value_heads)
    attended = out_heads.reshape(length, D)
    residual = stream + jnp.dot(attended, w_out, preferred_element_type=jnp.float32) + out_bias
    normed_two, inverse_two = normalize(residual)
    hidden_two = (normed_two * ln2_gain + ln2_bias).astype(jnp.bfloat16)
    pre_act = jnp.dot(hidden_two, w_up, preferred_element_type=jnp.float32) + up_bias
    activated_wide, gelu_slope = gelu_parts(pre_act)
    activated = activated_wide.astype(jnp.bfloat16)
    layer_out = (residual + jnp.dot(activated, w_down, preferred_element_type=jnp.float32) + down_bias).astype(jnp.bfloat16)
    grad_out = grad_rows.astype(jnp.float32)
    w_down_grad = jnp.dot(activated.T, grad_rows, preferred_element_type=jnp.float32)
    down_bias_grad = lax.optimization_barrier(jnp.sum(grad_out, axis=0))
    grad_pre = (jnp.dot(grad_rows, w_down.T, preferred_element_type=jnp.float32) * gelu_slope).astype(jnp.bfloat16)
    w_up_grad = jnp.dot(hidden_two.T, grad_pre, preferred_element_type=jnp.float32)
    up_bias_grad = lax.optimization_barrier(jnp.sum(grad_pre.astype(jnp.float32), axis=0))
    grad_hidden_two = jnp.dot(grad_pre, w_up.T, preferred_element_type=jnp.float32)
    ln2_gain_grad = lax.optimization_barrier(jnp.sum(grad_hidden_two * normed_two, axis=0))
    ln2_bias_grad = lax.optimization_barrier(jnp.sum(grad_hidden_two, axis=0))
    grad_residual = grad_out + norm_back(grad_hidden_two * ln2_gain, normed_two, inverse_two)
    grad_mixed = grad_residual.astype(jnp.bfloat16)
    w_out_grad = jnp.dot(attended.T, grad_mixed, preferred_element_type=jnp.float32)
    out_bias_grad = lax.optimization_barrier(jnp.sum(grad_mixed.astype(jnp.float32), axis=0))
    grad_attended = jnp.dot(grad_mixed, w_out.T, preferred_element_type=jnp.float32).astype(jnp.bfloat16)
    grad_queries, grad_keys, grad_values = attend_backward(query_heads, key_heads, value_heads, grad_attended.reshape(length, HEADS, HEAD_DIM), out_heads, log_rows)
    grad_proj = jnp.concatenate([grad_queries.reshape(length, D).astype(jnp.bfloat16), grad_keys.reshape(length, D).astype(jnp.bfloat16), grad_values.reshape(length, D).astype(jnp.bfloat16)], axis=1)
    w_qkv_grad = jnp.dot(hidden_one.T, grad_proj, preferred_element_type=jnp.float32)
    proj_wide = grad_proj.astype(jnp.float32)
    qv_bias_grad = jnp.stack([lax.optimization_barrier(jnp.sum(proj_wide[:, :D], axis=0)), lax.optimization_barrier(jnp.sum(proj_wide[:, 2 * D:], axis=0))])
    grad_hidden_one = jnp.dot(grad_proj, w_qkv.T, preferred_element_type=jnp.float32)
    ln1_gain_grad = lax.optimization_barrier(jnp.sum(grad_hidden_one * normed_one, axis=0))
    ln1_bias_grad = lax.optimization_barrier(jnp.sum(grad_hidden_one, axis=0))
    input_grad = (grad_residual + norm_back(grad_hidden_one * ln1_gain, normed_one, inverse_one)).astype(jnp.bfloat16)
    gradients = (ln1_gain_grad, ln1_bias_grad, w_qkv_grad, qv_bias_grad, w_out_grad, out_bias_grad, ln2_gain_grad, ln2_bias_grad, w_up_grad, up_bias_grad, w_down_grad, down_bias_grad)
    return (layer_out, input_grad, gradients)

def reference(layer_in, out_grad, block_order, ln1_gain, ln1_bias, w_qkv, qv_bias, w_out, out_bias, ln2_gain, ln2_bias, w_up, up_bias, w_down, down_bias):
    parameters = (ln1_gain, ln1_bias, w_qkv, qv_bias, w_out, out_bias, ln2_gain, ln2_bias, w_up, up_bias, w_down, down_bias)
    half_rows = LEN // SLOTS
    out_pieces = []
    grad_pieces = []
    totals = None
    for sequence in range(SEQS):
        order_row = block_order[sequence].astype(jnp.int32)
        seq_rows = layer_in[sequence].reshape(SLOTS, half_rows, D)
        seq_grad = out_grad[sequence].reshape(SLOTS, half_rows, D)
        natural_rows = jnp.zeros_like(seq_rows).at[order_row].set(seq_rows).reshape(LEN, D)
        natural_grad = jnp.zeros_like(seq_grad).at[order_row].set(seq_grad).reshape(LEN, D)
        out_natural, grad_natural, gradients = one_sequence(natural_rows, natural_grad, parameters)
        out_pieces.append(out_natural.reshape(SLOTS, half_rows, D)[order_row].reshape(LEN, D))
        grad_pieces.append(grad_natural.reshape(SLOTS, half_rows, D)[order_row].reshape(LEN, D))
        if totals is None:
            totals = gradients
        else:
            totals = jax.tree.map(lambda former, latter: former + latter, totals, gradients)
    layer_out = jnp.stack(out_pieces, axis=0)
    input_grad = jnp.stack(grad_pieces, axis=0)
    return (layer_out, input_grad, totals[0], totals[1], totals[2], totals[3], totals[4], totals[5], totals[6], totals[7], totals[8], totals[9], totals[10], totals[11])
```

```python
from functools import partial
import math

import jax
import jax.numpy as jnp
from jax import lax
from jax.experimental import pallas as pl
from jax.experimental.pallas import tpu as pltpu
from jax.sharding import PartitionSpec as P

HEADS = 25


EPS = 1e-05
GELU_C = 0.7978845608028654
NEG_FILL = -1e30
BF16 = jnp.bfloat16
F32 = jnp.float32


def normalize(row_data):
    centre = jnp.mean(row_data, axis=-1, keepdims=True)
    shifted = row_data - centre
    inverse = lax.rsqrt(jnp.mean(shifted * shifted, axis=-1, keepdims=True) + EPS)
    return (shifted * inverse, inverse)


def norm_back(grad_hat, normed, inverse):
    first_mean = jnp.mean(grad_hat, axis=-1, keepdims=True)
    second = jnp.mean(grad_hat * normed, axis=-1, keepdims=True)
    return inverse * (grad_hat - first_mean - normed * second)


def gelu_parts(values):
    cubic_term = 0.044715 * values * values * values
    tangent = jnp.tanh(GELU_C * (values + cubic_term))
    output = 0.5 * values * (1.0 + tangent)
    gelu_slope = 0.5 * (1.0 + tangent) + 0.5 * values * (1.0 - tangent * tangent) * GELU_C * (
        1.0 + 3.0 * 0.044715 * values * values
    )
    return (output, gelu_slope)


def head_parts(value, head_width):
    heads = value.shape[1] // head_width
    if heads == 1:
        return [value]
    lane = lax.broadcasted_iota(jnp.int32, value.shape, 1) // head_width
    return [jnp.where(lane == h, value, jnp.zeros_like(value)) for h in range(heads)]


def by_head(columns, shape, head_width):
    if len(columns) == 1:
        return jnp.broadcast_to(columns[0], shape)
    lane = lax.broadcasted_iota(jnp.int32, shape, 1) // head_width
    result = jnp.broadcast_to(columns[-1], shape)
    for h in range(len(columns) - 2, -1, -1):
        result = jnp.where(lane == h, columns[h], result)
    return result


def dot(a, b, contract):
    return lax.dot_general(a, b, (contract, ((), ())), preferred_element_type=F32)


def each_query_block(length, block, visit):
    if length // block <= 4:
        for index in range(length // block):
            chunks = [(0, index * block, False)] if index else []
            visit(index * block, chunks + [(index * block, block, True)])
    else:

        def step(index, carry):
            visit(pl.multiple_of(index * block, block), [(0, length, True)])
            return carry

        lax.fori_loop(0, length // block, step, 0)


def visible_mask(first_row, rows, first_key, keys):
    row_ids = first_row + lax.broadcasted_iota(jnp.int32, (rows, keys), 0)
    key_ids = first_key + lax.broadcasted_iota(jnp.int32, (rows, keys), 1)
    return key_ids <= row_ids


def forward_kernel(
    half, block, head_width, score_scale, order, qkv, slot_out, natural, out_rows, log_rows
):
    seq = pl.program_id(0)
    sources = qkv.shape[0]
    length = natural.shape[2]

    def place(source, carry):
        for part in range(2):
            first = pl.multiple_of(order[seq, 2 * source + part] * half, half)
            for kind in range(3):
                natural[kind, 0, pl.ds(first, half), :] = qkv[
                    source, kind, 0, part * half : (part + 1) * half, :
                ]
        return carry

    lax.fori_loop(0, sources, place, 0)

    def visit(first_row, chunks):
        rows = pl.ds(first_row, block)
        queries = natural[0, 0, rows, :] * jnp.asarray(score_scale, BF16)
        outputs = []
        logs = []
        for query in head_parts(queries, head_width):
            scores = []
            for first_key, keys, masked in chunks:
                part = dot(query, natural[1, 0, first_key : first_key + keys, :], ((1,), (1,)))
                if masked:
                    part = jnp.where(
                        visible_mask(first_row, block, first_key, keys), part, NEG_FILL
                    )
                scores.append(part)
            top = jnp.max(scores[0], axis=1, keepdims=True)
            for part in scores[1:]:
                top = jnp.maximum(top, jnp.max(part, axis=1, keepdims=True))
            total = jnp.zeros((block, 1), F32)
            summed = jnp.zeros((block, queries.shape[1]), F32)
            for (first_key, keys, masked), part in zip(chunks, scores):
                weights = jnp.exp(part - top)
                total = total + jnp.sum(weights, axis=1, keepdims=True)
                coarse = weights.astype(BF16)
                fine = (weights - coarse.astype(F32)).astype(BF16)
                values = natural[2, 0, first_key : first_key + keys, :]
                summed = summed + dot(coarse, values, ((1,), (0,))) + dot(fine, values, ((1,), (0,)))
            outputs.append(summed / total)
            logs.append(top + jnp.log(total))
        result = outputs[0]
        if len(outputs) > 1:
            lane = lax.broadcasted_iota(jnp.int32, result.shape, 1) // head_width
            for h in range(1, len(outputs)):
                result = jnp.where(lane == h, outputs[h], result)
        out_rows[0, rows, :] = result.astype(BF16)
        log_rows[0, rows, :] = by_head(logs, result.shape, head_width)

    each_query_block(length, block, visit)

    def give(source, carry):
        for part in range(2):
            first = pl.multiple_of(order[seq, 2 * source + part] * half, half)
            slot_out[source, 0, part * half : (part + 1) * half, :] = out_rows[
                0, pl.ds(first, half), :
            ]
        return carry

    lax.fori_loop(0, sources, give, 0)


def backward_kernel(
    half,
    block,
    head_width,
    score_scale,
    order,
    natural,
    out_rows,
    log_rows,
    grad_slots,
    slot_out,
    grad_rows,
    grad_queries,
    grad_keys,
    grad_values,
):
    seq = pl.program_id(0)
    sources = grad_slots.shape[0]
    length = natural.shape[2]

    def place(source, carry):
        for part in range(2):
            first = pl.multiple_of(order[seq, 2 * source + part] * half, half)
            grad_rows[pl.ds(first, half), :] = grad_slots[
                source, 0, part * half : (part + 1) * half, :
            ]
        return carry

    lax.fori_loop(0, sources, place, 0)
    grad_keys[...] = jnp.zeros_like(grad_keys)
    grad_values[...] = jnp.zeros_like(grad_values)

    def visit(first_row, chunks):
        rows = pl.ds(first_row, block)
        queries = natural[0, 0, rows, :] * jnp.asarray(score_scale, BF16)
        grads = grad_rows[rows, :]
        products = grads.astype(F32) * out_rows[0, rows, :].astype(F32)
        logs = log_rows[0, rows, :]
        query_sum = jnp.zeros(products.shape, F32)
        parts = zip(
            head_parts(queries, head_width),
            head_parts(grads, head_width),
            head_parts(products, head_width),
        )
        for h, (query, grad, product) in enumerate(parts):
            delta = jnp.sum(product, axis=1, keepdims=True)
            log_total = logs[:, h * head_width : h * head_width + 1]
            for first_key, keys, masked in chunks:
                span = slice(first_key, first_key + keys)
                key_block = natural[1, 0, span, :]
                scores = dot(query, key_block, ((1,), (1,)))
                probs = jnp.exp(scores - log_total)
                if masked:
                    probs = jnp.where(
                        visible_mask(first_row, block, first_key, keys), probs, 0.0
                    )
                grad_probs = dot(grad, natural[2, 0, span, :], ((1,), (1,)))
                grad_scores = (probs * (grad_probs - delta)).astype(BF16)
                grad_values[span, :] += dot(probs.astype(BF16), grad, ((0,), (0,)))
                grad_keys[span, :] += dot(grad_scores, query, ((0,), (0,)))
                query_sum = query_sum + dot(
                    grad_scores, head_parts(key_block, head_width)[h], ((1,), (0,))
                )
        grad_queries[rows, :] = query_sum * score_scale

    each_query_block(length, block, visit)

    def give(source, carry):
        for part in range(2):
            first = pl.multiple_of(order[seq, 2 * source + part] * half, half)
            to_rows = slice(part * half, (part + 1) * half)
            for kind, rows in enumerate((grad_queries, grad_keys, grad_values)):
                slot_out[source, kind, 0, to_rows, :] = rows[pl.ds(first, half), :].astype(BF16)
        return carry

    lax.fori_loop(0, sources, give, 0)


def attend_forward(qkv, order, head_width, score_scale):
    sources, kinds, seqs, rows, lanes = qkv.shape
    length = sources * rows
    block = math.gcd(length, 256)
    return pl.pallas_call(
        partial(forward_kernel, rows // 2, block, head_width, score_scale),
        grid_spec=pltpu.PrefetchScalarGridSpec(
            num_scalar_prefetch=1,
            grid=(seqs,),
            in_specs=[pl.BlockSpec((sources, 3, 1, rows, lanes), lambda s, o: (0, 0, s, 0, 0))],
            out_specs=[
                pl.BlockSpec((sources, 1, rows, lanes), lambda s, o: (0, s, 0, 0)),
                pl.BlockSpec((3, 1, length, lanes), lambda s, o: (0, s, 0, 0)),
                pl.BlockSpec((1, length, lanes), lambda s, o: (s, 0, 0)),
                pl.BlockSpec((1, length, lanes), lambda s, o: (s, 0, 0)),
            ],
        ),
        out_shape=[
            jax.ShapeDtypeStruct((sources, seqs, rows, lanes), BF16),
            jax.ShapeDtypeStruct((3, seqs, length, lanes), BF16),
            jax.ShapeDtypeStruct((seqs, length, lanes), BF16),
            jax.ShapeDtypeStruct((seqs, length, lanes), F32),
        ],
        name="attend_forward",
    )(order, qkv)


def attend_backward(natural, out_rows, log_rows, grad_slots, order, head_width, score_scale):
    sources, seqs, rows, lanes = grad_slots.shape
    length = sources * rows
    block = math.gcd(length, 256)
    return pl.pallas_call(
        partial(backward_kernel, rows // 2, block, head_width, score_scale),
        grid_spec=pltpu.PrefetchScalarGridSpec(
            num_scalar_prefetch=1,
            grid=(seqs,),
            in_specs=[
                pl.BlockSpec((3, 1, length, lanes), lambda s, o: (0, s, 0, 0)),
                pl.BlockSpec((1, length, lanes), lambda s, o: (s, 0, 0)),
                pl.BlockSpec((1, length, lanes), lambda s, o: (s, 0, 0)),
                pl.BlockSpec((sources, 1, rows, lanes), lambda s, o: (0, s, 0, 0)),
            ],
            out_specs=[
                pl.BlockSpec((sources, 3, 1, rows, lanes), lambda s, o: (0, 0, s, 0, 0)),
            ],
            scratch_shapes=[
                pltpu.VMEM((length, lanes), BF16),
                pltpu.VMEM((length, lanes), F32),
                pltpu.VMEM((length, lanes), F32),
                pltpu.VMEM((length, lanes), F32),
            ],
        ),
        out_shape=[jax.ShapeDtypeStruct((sources, 3, seqs, rows, lanes), BF16)],
        name="attend_backward",
    )(order, natural, out_rows, log_rows, grad_slots)[0]


def to_heads(rows, devices, seqs, lanes):
    tokens, width = rows.shape
    padded = jnp.pad(rows, ((0, 0), (0, devices * lanes - width)))
    return jnp.transpose(padded.reshape(seqs, tokens // seqs, devices, lanes), (2, 0, 1, 3))


def from_heads(blocks, width):
    devices, seqs, rows, lanes = blocks.shape
    joined = jnp.transpose(blocks, (1, 2, 0, 3)).reshape(seqs * rows, devices * lanes)
    return joined[:, :width]


def shards(
    ctx,
    layer_in,
    out_grad,
    block_order,
    ln1_gain,
    ln1_bias,
    w_qkv,
    qv_bias,
    w_out,
    out_bias,
    ln2_gain,
    ln2_bias,
    w_up,
    up_bias,
    w_down,
    down_bias,
):
    seqs, tok_rows, width = layer_in.shape
    tokens = seqs * tok_rows
    head_width = width // HEADS
    score_scale = 1.0 / math.sqrt(head_width)
    lanes = -(-HEADS // ctx) * head_width
    half_units = w_up.shape[1]
    half_cols = w_out.shape[1]
    half_proj = w_qkv.shape[1]
    my_dp = lax.axis_index("dp")
    my_core = lax.axis_index("ctx") % 2
    core_swap = [(i, i ^ 1) for i in range(ctx)]

    def across(x):
        return lax.ppermute(x, "dp", [(0, 1), (1, 0)])

    def after(x, *earlier):
        return lax.optimization_barrier((x,) + earlier)[0]

    def by_dp(mine, other):
        return jnp.where(my_dp == 0, mine, other), jnp.where(my_dp == 0, other, mine)

    def fetch(send):
        rows = send.shape[0] // 2
        part = across(lax.dynamic_slice_in_dim(send, my_core * rows, rows, 0))
        rest = lax.ppermute(part, "ctx", core_swap)
        low = jnp.where(my_core == 0, part, rest)
        high = jnp.where(my_core == 0, rest, part)
        return jnp.concatenate([low, high], axis=0)

    own_in = layer_in.reshape(tokens, width)
    own_out_grad = out_grad.reshape(tokens, width)
    other_in = across(own_in)
    stream = own_in.astype(F32)
    normed_one, inverse_one = normalize(stream)
    hidden_one = (normed_one * ln1_gain + ln1_bias).astype(BF16)
    hidden_one_other = (normalize(other_in.astype(F32))[0] * ln1_gain + ln1_bias).astype(BF16)
    proj_bias = jnp.concatenate([qv_bias[0], jnp.zeros_like(qv_bias[0]), qv_bias[1]])
    proj_bias = lax.dynamic_slice_in_dim(proj_bias, my_dp * half_proj, half_proj, 0)
    proj_other = (
        jnp.dot(hidden_one_other, w_qkv, preferred_element_type=F32) + proj_bias
    ).astype(BF16)
    proj_got = across(proj_other)
    proj_own = (jnp.dot(hidden_one, w_qkv, preferred_element_type=F32) + proj_bias).astype(BF16)
    low, high = by_dp(proj_own, proj_got)
    queries = low[:, :width]
    keys = jnp.concatenate([low[:, width:], high[:, : 2 * width - half_proj]], axis=1)
    values = high[:, 2 * width - half_proj :]
    send = jnp.stack([to_heads(x, ctx, seqs, lanes) for x in (queries, keys, values)], axis=1)
    qkv_heads = lax.all_to_all(send, "ctx", 0, 0, tiled=True)

    other_out_grad = across(after(own_out_grad, proj_got))
    w_out_other = fetch(after(w_out, proj_got))
    out_low, out_high = by_dp(w_out, w_out_other)
    unit_rows = w_down.shape[0] // 2
    down_mine = lax.dynamic_slice_in_dim(w_down, my_dp * unit_rows, unit_rows, 0)
    down_send = lax.dynamic_slice_in_dim(w_down, (1 - my_dp) * unit_rows, unit_rows, 0)
    down_other = fetch(after(down_send, w_out_other))
    down_low, down_high = by_dp(down_mine, down_other)

    hidden_one_all = lax.all_gather(after(hidden_one, qkv_heads), "ctx", axis=0, tiled=True)

    attended_slots, natural, out_rows, log_rows = attend_forward(
        qkv_heads, block_order, head_width, score_scale
    )
    attended = from_heads(lax.all_to_all(attended_slots, "ctx", 0, 0, tiled=True), width)

    mixed = jnp.concatenate(
        [
            jnp.dot(attended, out_low, preferred_element_type=F32),
            jnp.dot(attended, out_high, preferred_element_type=F32),
        ],
        axis=1,
    )
    residual = stream + mixed + out_bias
    normed_two, inverse_two = normalize(residual)
    hidden_two = (normed_two * ln2_gain + ln2_bias).astype(BF16)
    hidden_two_pair = jnp.concatenate([hidden_two, across(hidden_two)], axis=0)
    out_grad_pair = jnp.concatenate([own_out_grad, other_out_grad], axis=0)

    up_half = lax.dynamic_slice_in_dim(up_bias, my_dp * half_units, half_units, 0)
    grad_active = jnp.einsum(
        "td,fd->tf", out_grad_pair[:, :half_cols], down_low, preferred_element_type=F32
    ) + jnp.einsum("td,fd->tf", out_grad_pair[:, half_cols:], down_high, preferred_element_type=F32)
    pre_act = jnp.dot(hidden_two_pair, w_up, preferred_element_type=F32) + up_half
    activated_wide, gelu_slope = gelu_parts(pre_act)
    activated = activated_wide.astype(BF16)
    grad_pre = (grad_active * gelu_slope).astype(BF16)
    grad_two = jnp.einsum("tf,df->td", grad_pre, w_up, preferred_element_type=F32)
    grad_two_got = across(grad_two[tokens:].astype(BF16))
    grad_hidden_two = grad_two[:tokens] + grad_two_got.astype(F32)
    down_sum = jnp.concatenate(
        [
            jnp.dot(activated, down_low, preferred_element_type=F32),
            jnp.dot(activated, down_high, preferred_element_type=F32),
        ],
        axis=1,
    )
    down_got = across(after(down_sum[tokens:].astype(BF16), grad_two_got))
    layer_out = (residual + (down_sum[:tokens] + down_got.astype(F32)) + down_bias).astype(BF16)

    blocks = ctx // 2
    unit_block = half_units // blocks
    down_part = jnp.einsum("tf,td->fd", activated, out_grad_pair, preferred_element_type=F32)
    down_part = jnp.transpose(
        down_part.astype(BF16).reshape(blocks, unit_block, 2, half_cols), (2, 0, 1, 3)
    ).reshape(ctx, unit_block, half_cols)
    up_part = jnp.einsum("td,tf->df", hidden_two_pair, grad_pre, preferred_element_type=F32)
    up_part = jnp.transpose(
        up_part.astype(BF16).reshape(2, half_cols, blocks, unit_block), (0, 2, 1, 3)
    ).reshape(ctx, half_cols, unit_block)
    owner = [
        (d * ctx + e * blocks + j, e * ctx + d * blocks + j)
        for d in range(2)
        for e in range(2)
        for j in range(blocks)
    ]
    down_grad = lax.psum_scatter(down_part, "ctx", scatter_dimension=0, tiled=False)
    up_grad = lax.psum_scatter(up_part, "ctx", scatter_dimension=0, tiled=False)
    down_grad = lax.ppermute(down_grad, ("dp", "ctx"), owner).astype(F32)
    up_grad = lax.ppermute(up_grad, ("dp", "ctx"), owner).astype(F32)

    grad_out = own_out_grad.astype(F32)
    grad_residual = grad_out + norm_back(grad_hidden_two * ln2_gain, normed_two, inverse_two)
    grad_mixed = grad_residual.astype(BF16)
    grad_attended = (
        jnp.einsum("tb,ab->ta", grad_mixed[:, :half_cols], out_low, preferred_element_type=F32)
        + jnp.einsum("tb,ab->ta", grad_mixed[:, half_cols:], out_high, preferred_element_type=F32)
    ).astype(BF16)
    grad_slots = lax.all_to_all(
        to_heads(grad_attended, ctx, seqs, lanes), "ctx", 0, 0, tiled=True
    )
    mixed_all = lax.all_gather(after(grad_mixed, grad_slots), "ctx", axis=0, tiled=True)
    qkv_other = fetch(after(w_qkv.T, grad_two_got))
    qkv_low, qkv_high = by_dp(w_qkv.T, qkv_other)
    proj_slots = attend_backward(
        natural, out_rows, log_rows, grad_slots, block_order, head_width, score_scale
    )
    proj_back = lax.all_to_all(proj_slots, "ctx", 0, 0, tiled=True)
    grad_proj = jnp.concatenate(
        [from_heads(proj_back[:, kind], width) for kind in range(3)], axis=1
    )
    grad_hidden_one = jnp.dot(
        grad_proj[:, :half_proj], qkv_low, preferred_element_type=F32
    ) + jnp.dot(grad_proj[:, half_proj:], qkv_high, preferred_element_type=F32)
    input_grad = (
        grad_residual + norm_back(grad_hidden_one * ln1_gain, normed_one, inverse_one)
    ).astype(BF16)

    def columns(rows):
        return jnp.transpose(rows.reshape(tokens, ctx, -1), (1, 0, 2))

    proj_cols = lax.all_to_all(columns(grad_proj), "ctx", 0, 0, tiled=True)
    proj_cols = proj_cols.reshape(ctx * tokens, -1)
    attended_cols = lax.all_to_all(columns(attended), "ctx", 0, 0, tiled=True)
    attended_cols = attended_cols.reshape(ctx * tokens, -1)
    qkv_part = jnp.einsum("td,tc->dc", hidden_one_all, proj_cols, preferred_element_type=F32)
    out_part = jnp.einsum("tc,td->cd", attended_cols, mixed_all, preferred_element_type=F32)

    def keep_and_send(part, axis):
        size = part.shape[axis] // 2
        kept = lax.dynamic_slice_in_dim(part, my_dp * size, size, axis)
        sent = lax.dynamic_slice_in_dim(part, (1 - my_dp) * size, size, axis).astype(BF16)
        return kept + across(sent).astype(F32)

    qkv_grad = keep_and_send(qkv_part, 0)
    out_weight_grad = keep_and_send(out_part, 1)

    up_sums = jnp.sum(grad_pre.astype(F32), axis=0)
    none = jnp.zeros_like(up_sums)
    up_sums = jnp.concatenate(
        [jnp.where(my_dp == 0, up_sums, none), jnp.where(my_dp == 0, none, up_sums)]
    )
    proj_sums = jnp.sum(grad_proj.astype(F32), axis=0)
    sums = [
        jnp.sum(grad_hidden_one * normed_one, axis=0),
        jnp.sum(grad_hidden_one, axis=0),
        proj_sums[:width],
        proj_sums[2 * width :],
        jnp.sum(grad_mixed.astype(F32), axis=0),
        jnp.sum(grad_hidden_two * normed_two, axis=0),
        jnp.sum(grad_hidden_two, axis=0),
        jnp.sum(grad_out, axis=0),
        up_sums,
    ]
    packed = jnp.concatenate(sums)
    devices = 2 * ctx
    size = -(-packed.shape[0] // (devices * 128)) * 128
    count = packed.shape[0]
    packed = jnp.pad(packed, (0, devices * size - count)).reshape(devices, size // 128, 128)
    mine = jnp.sum(lax.all_to_all(packed, ("dp", "ctx"), 0, 0, tiled=True), axis=0)
    spread = jnp.broadcast_to(mine[None], (devices,) + mine.shape)
    totals = lax.all_to_all(spread, ("dp", "ctx"), 0, 0, tiled=True).reshape(-1)
    pieces = []
    first = 0
    for item in sums:
        pieces.append(totals[first : first + item.shape[0]])
        first += item.shape[0]

    return (
        layer_out.reshape(layer_in.shape),
        input_grad.reshape(layer_in.shape),
        pieces[0],
        pieces[1],
        qkv_grad,
        jnp.stack([pieces[2], pieces[3]]),
        out_weight_grad,
        pieces[4],
        pieces[5],
        pieces[6],
        up_grad,
        pieces[8],
        down_grad,
        pieces[7],
    )


def solution(mesh):
    placed = (
        P("dp", "ctx", None),
        P("dp", "ctx", None),
        P("dp", None),
        P(),
        P(),
        P(None, "dp"),
        P(),
        P(None, "dp"),
        P(),
        P(),
        P(),
        P(None, "dp"),
        P(),
        P(None, "dp"),
        P(),
    )
    return jax.shard_map(
        partial(shards, mesh.shape["ctx"]),
        mesh=mesh,
        in_specs=placed,
        out_specs=(
            P("dp", "ctx", None),
            P("dp", "ctx", None),
            P(),
            P(),
            P("dp", "ctx"),
            P(),
            P("ctx", "dp"),
            P(),
            P(),
            P(),
            P("dp", "ctx"),
            P(),
            P("ctx", "dp"),
            P(),
        ),
        check_vma=False,
    )
```

```python
from functools import partial
import math

import jax
import jax.numpy as jnp
from jax import lax
from jax.experimental import pallas as pl
from jax.experimental.pallas import tpu as pltpu
from jax.sharding import PartitionSpec as P

from jax.experimental.layout import Layout, with_layout_constraint

HEADS = 25


EPS = 1e-05
GELU_C = 0.7978845608028654
NEG_FILL = -1e30
BF16 = jnp.bfloat16
F32 = jnp.float32


def normalize(data):
    centre = jnp.mean(data, axis=0, keepdims=True)
    shifted = data - centre
    inverse = lax.rsqrt(jnp.mean(shifted * shifted, axis=0, keepdims=True) + EPS)
    return (shifted * inverse, inverse)


def norm_back(grad_hat, normed, inverse):
    first_mean = jnp.mean(grad_hat, axis=0, keepdims=True)
    second = jnp.mean(grad_hat * normed, axis=0, keepdims=True)
    return inverse * (grad_hat - first_mean - normed * second)


def gelu_parts(values):
    cubic_term = 0.044715 * values * values * values
    tangent = jnp.tanh(GELU_C * (values + cubic_term))
    output = 0.5 * values * (1.0 + tangent)
    gelu_slope = 0.5 * (1.0 + tangent) + 0.5 * values * (1.0 - tangent * tangent) * GELU_C * (
        1.0 + 3.0 * 0.044715 * values * values
    )
    return (output, gelu_slope)


def head_parts(value, head_width):
    heads = value.shape[1] // head_width
    if heads == 1:
        return [value]
    lane = lax.broadcasted_iota(jnp.int32, value.shape, 1) // head_width
    return [jnp.where(lane == h, value, jnp.zeros_like(value)) for h in range(heads)]


def by_head(columns, shape, head_width):
    if len(columns) == 1:
        return jnp.broadcast_to(columns[0], shape)
    lane = lax.broadcasted_iota(jnp.int32, shape, 1) // head_width
    result = jnp.broadcast_to(columns[-1], shape)
    for h in range(len(columns) - 2, -1, -1):
        result = jnp.where(lane == h, columns[h], result)
    return result


def dot(a, b, contract):
    return lax.dot_general(a, b, (contract, ((), ())), preferred_element_type=F32)


def each_query_block(length, block, visit):
    if length // block <= 4:
        for index in range(length // block):
            chunks = [(0, index * block, False)] if index else []
            visit(index * block, chunks + [(index * block, block, True)])
    else:

        def step(index, carry):
            visit(pl.multiple_of(index * block, block), [(0, length, True)])
            return carry

        lax.fori_loop(0, length // block, step, 0)


def visible_mask(first_row, rows, first_key, keys):
    row_ids = first_row + lax.broadcasted_iota(jnp.int32, (rows, keys), 0)
    key_ids = first_key + lax.broadcasted_iota(jnp.int32, (rows, keys), 1)
    return key_ids <= row_ids


def slot_rows(order, seq, source, half):
    return [pl.multiple_of(order[seq, 2 * source + part] * half, half) for part in range(2)]


def forward_kernel(
    half, block, head_width, score_scale, order, qkv, slot_out, natural, out_rows, log_rows
):
    sources = qkv.shape[0]
    kinds, seqs, length, lanes = natural.shape

    def place(source, carry):
        for kind in range(kinds):
            rows = qkv[source, kind].T
            for seq in range(seqs):
                for part, first in enumerate(slot_rows(order, seq, source, half)):
                    begin = (2 * seq + part) * half
                    natural[kind, seq, pl.ds(first, half), :] = rows[begin : begin + half, :]
        return carry

    lax.fori_loop(0, sources, place, 0)

    def visit(seq, first_row, chunks):
        rows = pl.ds(first_row, block)
        queries = natural[0, seq, rows, :] * jnp.asarray(score_scale, BF16)
        outputs = []
        logs = []
        for query in head_parts(queries, head_width):
            scores = []
            for first_key, keys, masked in chunks:
                part = dot(query, natural[1, seq, first_key : first_key + keys, :], ((1,), (1,)))
                if masked:
                    part = jnp.where(
                        visible_mask(first_row, block, first_key, keys), part, NEG_FILL
                    )
                scores.append(part)
            top = jnp.max(scores[0], axis=1, keepdims=True)
            for part in scores[1:]:
                top = jnp.maximum(top, jnp.max(part, axis=1, keepdims=True))
            total = jnp.zeros((block, 1), F32)
            summed = jnp.zeros((block, lanes), F32)
            for (first_key, keys, masked), part in zip(chunks, scores):
                weights = jnp.exp(part - top)
                total = total + jnp.sum(weights, axis=1, keepdims=True)
                coarse = weights.astype(BF16)
                fine = (weights - coarse.astype(F32)).astype(BF16)
                values = natural[2, seq, first_key : first_key + keys, :]
                summed = summed + dot(coarse, values, ((1,), (0,))) + dot(fine, values, ((1,), (0,)))
            outputs.append(summed / total)
            logs.append(top + jnp.log(total))
        result = outputs[0]
        if len(outputs) > 1:
            lane = lax.broadcasted_iota(jnp.int32, result.shape, 1) // head_width
            for h in range(1, len(outputs)):
                result = jnp.where(lane == h, outputs[h], result)
        out_rows[seq, rows, :] = result.astype(BF16)
        log_rows[seq, rows, :] = by_head(logs, result.shape, head_width)

    def one_sequence(seq, carry):
        each_query_block(length, block, partial(visit, seq))
        return carry

    lax.fori_loop(0, seqs, one_sequence, 0)

    def give(source, carry):
        rows = [
            out_rows[seq, pl.ds(first, half), :]
            for seq in range(seqs)
            for first in slot_rows(order, seq, source, half)
        ]
        slot_out[source] = jnp.concatenate(rows, axis=0).T
        return carry

    lax.fori_loop(0, sources, give, 0)


def backward_kernel(
    half,
    block,
    head_width,
    score_scale,
    order,
    natural,
    out_rows,
    log_rows,
    grad_slots,
    slot_out,
    grad_rows,
    grad_natural,
):
    sources = grad_slots.shape[0]
    kinds, seqs, length, lanes = natural.shape

    def place(source, carry):
        rows = grad_slots[source].T
        for seq in range(seqs):
            for part, first in enumerate(slot_rows(order, seq, source, half)):
                begin = (2 * seq + part) * half
                grad_rows[seq, pl.ds(first, half), :] = rows[begin : begin + half, :]
        return carry

    lax.fori_loop(0, sources, place, 0)
    grad_natural[1:] = jnp.zeros((kinds - 1, seqs, length, lanes), F32)

    def visit(seq, first_row, chunks):
        rows = pl.ds(first_row, block)
        queries = natural[0, seq, rows, :] * jnp.asarray(score_scale, BF16)
        grads = grad_rows[seq, rows, :]
        products = grads.astype(F32) * out_rows[seq, rows, :].astype(F32)
        logs = log_rows[seq, rows, :]
        query_sum = jnp.zeros(products.shape, F32)
        parts = zip(
            head_parts(queries, head_width),
            head_parts(grads, head_width),
            head_parts(products, head_width),
        )
        for h, (query, grad, product) in enumerate(parts):
            delta = jnp.sum(product, axis=1, keepdims=True)
            log_total = logs[:, h * head_width : h * head_width + 1]
            for first_key, keys, masked in chunks:
                span = slice(first_key, first_key + keys)
                key_block = natural[1, seq, span, :]
                scores = dot(query, key_block, ((1,), (1,)))
                probs = jnp.exp(scores - log_total)
                if masked:
                    probs = jnp.where(
                        visible_mask(first_row, block, first_key, keys), probs, 0.0
                    )
                grad_probs = dot(grad, natural[2, seq, span, :], ((1,), (1,)))
                grad_scores = (probs * (grad_probs - delta)).astype(BF16)
                grad_natural[2, seq, span, :] += dot(probs.astype(BF16), grad, ((0,), (0,)))
                grad_natural[1, seq, span, :] += dot(grad_scores, query, ((0,), (0,)))
                query_sum = query_sum + dot(
                    grad_scores, head_parts(key_block, head_width)[h], ((1,), (0,))
                )
        grad_natural[0, seq, rows, :] = query_sum * score_scale

    def one_sequence(seq, carry):
        each_query_block(length, block, partial(visit, seq))
        return carry

    lax.fori_loop(0, seqs, one_sequence, 0)

    def give(source, carry):
        for kind in range(kinds):
            rows = [
                grad_natural[kind, seq, pl.ds(first, half), :]
                for seq in range(seqs)
                for first in slot_rows(order, seq, source, half)
            ]
            slot_out[source, kind] = jnp.concatenate(rows, axis=0).astype(BF16).T
        return carry

    lax.fori_loop(0, sources, give, 0)


def in_vmem(count):
    return [pl.BlockSpec(memory_space=pltpu.VMEM)] * count


def attend_forward(qkv, order, head_width, score_scale):
    sources, kinds, lanes, tokens = qkv.shape
    seqs = order.shape[0]
    length = sources * tokens // seqs
    block = math.gcd(length, 256)
    return pl.pallas_call(
        partial(forward_kernel, tokens // seqs // 2, block, head_width, score_scale),
        in_specs=[pl.BlockSpec(memory_space=pltpu.SMEM)] + in_vmem(1),
        out_specs=in_vmem(4),
        out_shape=[
            jax.ShapeDtypeStruct((sources, lanes, tokens), BF16),
            jax.ShapeDtypeStruct((kinds, seqs, length, lanes), BF16),
            jax.ShapeDtypeStruct((seqs, length, lanes), BF16),
            jax.ShapeDtypeStruct((seqs, length, lanes), F32),
        ],
        name="attf",
    )(order, qkv)


def attend_backward(natural, out_rows, log_rows, grad_slots, order, head_width, score_scale):
    sources, lanes, tokens = grad_slots.shape
    kinds, seqs, length, lanes = natural.shape
    block = math.gcd(length, 256)
    return pl.pallas_call(
        partial(backward_kernel, tokens // seqs // 2, block, head_width, score_scale),
        in_specs=[pl.BlockSpec(memory_space=pltpu.SMEM)] + in_vmem(4),
        out_specs=in_vmem(1)[0],
        scratch_shapes=[
            pltpu.VMEM((seqs, length, lanes), BF16),
            pltpu.VMEM((kinds, seqs, length, lanes), F32),
        ],
        out_shape=jax.ShapeDtypeStruct((sources, kinds, lanes, tokens), BF16),
        name="attb",
    )(order, natural, out_rows, log_rows, grad_slots)


def product_kernel(kept, got, own, side, core, parts):
    units, tokens = kept.shape[0], own.shape[1]
    halves, _, width = parts.shape
    block = own.shape[0] // halves
    pairs = (
        (kept, 0, own, 0),
        (kept, tokens, core, 0),
        (got, 0, side, 0),
        (got, tokens, core, tokens),
    )
    step = units // 2

    def one_half(half, carry):
        for first in range(0, units, step):
            total = jnp.zeros((step, block), F32)
            for left, left_at, right, right_at in pairs:
                a = left[first : first + step, left_at : left_at + tokens]
                rows = pl.ds(pl.multiple_of(half * block, 16), block)
                b = right[rows, right_at : right_at + tokens]
                total = total + dot(a, b, ((1,), (1,)))
            parts[half, first : first + step, :block] = total.astype(BF16)
            if width > block:
                blank = jnp.zeros((step, width - block), BF16)
                parts[half, first : first + step, block:] = blank
        return carry

    lax.fori_loop(0, halves, one_half, 0)


def tokens_product(units, rows):
    kept, got = units
    own, side, core = rows
    width = own.shape[0] // 2
    return pl.pallas_call(
        product_kernel,
        in_specs=in_vmem(5),
        out_specs=in_vmem(1)[0],
        out_shape=jax.ShapeDtypeStruct((2, kept.shape[0], width + -width % 128), BF16),
        name="prod",
    )(kept, got, own, side, core)


def rounds_of(edges):
    at_source, at_target = {}, {}
    for source, target, item in edges:
        sends, gets = at_source.setdefault(source, {}), at_target.setdefault(target, {})
        first = next(r for r in range(len(edges)) if r not in sends)
        last = next(r for r in range(len(edges)) if r not in gets)
        if first != last:
            path, node, side, look = [], target, at_target, first
            while look in side.setdefault(node, {}):
                edge = side[node][look]
                path.append((edge, look))
                node = edge[0] if side is at_target else edge[1]
                side = at_source if side is at_target else at_target
                look = first + last - look
            for edge, was in path:
                del at_source[edge[0]][was], at_target[edge[1]][was]
            for edge, was in path:
                now = first + last - was
                at_source[edge[0]][now] = at_target[edge[1]][now] = edge
        sends[first] = gets[first] = (source, target, item)
    count = 1 + max(r for sends in at_source.values() for r in sends)
    return [[sends[r] for sends in at_source.values() if r in sends] for r in range(count)]


def to_heads(data, devices, lanes):
    width, tokens = data.shape
    return jnp.pad(data, ((0, devices * lanes - width), (0, 0))).reshape(devices, lanes, tokens)


def from_heads(blocks, width):
    devices, lanes, tokens = blocks.shape
    return blocks.reshape(devices * lanes, tokens)[:width]


def shards(
    ctx,
    layer_in,
    out_grad,
    block_order,
    ln1_gain,
    ln1_bias,
    w_qkv,
    qv_bias,
    w_out,
    out_bias,
    ln2_gain,
    ln2_bias,
    w_up,
    up_bias,
    w_down,
    down_bias,
):
    seqs, tok_rows, width = layer_in.shape
    tokens = seqs * tok_rows
    head_width = width // HEADS
    score_scale = 1.0 / math.sqrt(head_width)
    lanes = -(-HEADS // ctx) * head_width
    half_units = w_up.shape[1]
    half_cols = w_out.shape[1]
    half_proj = w_qkv.shape[1]
    planes = ctx // 4
    my_dp = lax.axis_index("dp")
    my_ctx = lax.axis_index("ctx")
    my_core = my_ctx % 2
    my_side = (my_ctx // 2) % 2
    core_swap = [(i, i ^ 1) for i in range(ctx)]
    side_swap = [(i, i ^ 2) for i in range(ctx)]
    lines = [[q + 4 * z for z in range(planes)] for q in range(4)]

    def across(x):
        return lax.ppermute(x, "dp", [(0, 1), (1, 0)])

    def to_core(x):
        return lax.ppermute(x, "ctx", core_swap)

    def to_side(x):
        return lax.ppermute(x, "ctx", side_swap)

    def exchange(x):
        return lax.all_to_all(x, "ctx", 0, 0, tiled=True)

    def after(x, *earlier):
        return lax.optimization_barrier((x,) + earlier)[0]

    def pick(x, index, axis, count=2):
        size = x.shape[axis] // count
        return lax.dynamic_slice_in_dim(x, index * size, size, axis)

    def split(x, index, axis):
        return pick(x, index, axis), pick(x, 1 - index, axis)

    def joined(index, mine, other, axis=0):
        return jnp.where(
            index == 0,
            jnp.concatenate([mine, other], axis=axis),
            jnp.concatenate([other, mine], axis=axis),
        )

    def dot32(a, b, spec):
        return jnp.einsum(spec, a, b, preferred_element_type=F32)

    column = lambda vector: vector[:, None]

    own_in = layer_in.reshape(tokens, width).T
    own_out_grad = out_grad.reshape(tokens, width).T
    other_in = across(own_in)
    stream = own_in.astype(F32)
    normed_one, inverse_one = normalize(stream)
    gain_one, bias_one = column(ln1_gain), column(ln1_bias)
    hidden_one = (normed_one * gain_one + bias_one).astype(BF16)
    hidden_one_other = (normalize(other_in.astype(F32))[0] * gain_one + bias_one).astype(BF16)
    proj_bias = jnp.concatenate([qv_bias[0], jnp.zeros_like(qv_bias[0]), qv_bias[1]])
    proj_bias = column(pick(proj_bias, my_dp, 0))
    proj_other = (dot32(w_qkv, hidden_one_other, "de,dt->et") + proj_bias).astype(BF16)
    proj_got = across(proj_other)
    proj_own = (dot32(w_qkv, hidden_one, "de,dt->et") + proj_bias).astype(BF16)
    proj_own = lax.optimization_barrier(proj_own)
    low = jnp.where(my_dp == 0, proj_own, proj_got)
    high = jnp.where(my_dp == 0, proj_got, proj_own)
    queries = low[:width]
    keys = jnp.concatenate([low[width:], high[: 2 * width - half_proj]], axis=0)
    values = high[2 * width - half_proj :]
    send = jnp.stack([to_heads(x, ctx, lanes) for x in (queries, keys, values)], axis=1)
    qkv_heads = exchange(send)

    out_mine = across(after(pick(w_out, my_core, 0), proj_got))
    other_out_grad = across(after(own_out_grad, proj_got))
    down_rows = pick(w_down, my_dp, 0)
    down_send = pick(pick(w_down, 1 - my_dp, 0), my_core, 1)
    down_mine = across(after(down_send, proj_got))
    out_rest = to_core(after(out_mine, qkv_heads))

    hidden_one_all = lax.all_gather(after(hidden_one.T, qkv_heads), "ctx", axis=0, tiled=True)

    attended_slots, natural, out_rows, log_rows = attend_forward(
        qkv_heads, block_order, head_width, score_scale
    )
    attended = from_heads(exchange(attended_slots), width)
    down_rest = to_core(after(down_mine, attended))

    attended_mine, attended_rest = split(attended, my_core, 0)
    mixed = joined(
        my_dp,
        dot32(w_out, attended, "ab,at->bt"),
        dot32(out_mine, attended_mine, "ab,at->bt") + dot32(out_rest, attended_rest, "ab,at->bt"),
    )
    residual = stream + mixed + column(out_bias)
    normed_two, inverse_two = normalize(residual)
    gain_two = column(ln2_gain)
    hidden_two = (normed_two * gain_two + column(ln2_bias)).astype(BF16)
    hidden_two_pair = jnp.concatenate([hidden_two, across(hidden_two)], axis=1)

    out_grad_pair = after(
        jnp.concatenate([own_out_grad, after(other_out_grad, attended)], axis=1), hidden_two
    )
    out_grad_own, out_grad_rest = split(out_grad_pair, my_dp, 0)
    rest_mine, rest_rest = split(out_grad_rest, my_core, 0)
    grad_active = (
        dot32(down_rows, out_grad_own, "fd,dt->ft")
        + dot32(down_mine, rest_mine, "fd,dt->ft")
        + dot32(down_rest, rest_rest, "fd,dt->ft")
    )
    pre_act = dot32(w_up, hidden_two_pair, "df,dt->ft") + column(pick(up_bias, my_dp, 0))
    activated_wide, gelu_slope = gelu_parts(pre_act)
    activated = with_layout_constraint(activated_wide.astype(BF16), Layout((0, 1)))
    grad_pre = with_layout_constraint((grad_active * gelu_slope).astype(BF16), Layout((0, 1)))
    grad_two = dot32(grad_pre, w_up, "ft,df->dt")
    two_send = grad_two[:, tokens:].astype(BF16)
    grad_two_got = across(two_send)
    grad_hidden_two = grad_two[:, :tokens] + grad_two_got.astype(F32)

    grad_out = own_out_grad.astype(F32)
    grad_residual = grad_out + norm_back(grad_hidden_two * gain_two, normed_two, inverse_two)
    grad_mixed = grad_residual.astype(BF16)
    mixed_own, mixed_other = split(grad_mixed, my_dp, 0)
    grad_attended = (
        dot32(w_out, mixed_own, "ab,bt->at")
        + joined(
            my_core,
            dot32(out_mine, mixed_other, "ab,bt->at"),
            dot32(out_rest, mixed_other, "ab,bt->at"),
        )
    ).astype(BF16)
    middle_sums = [
        jnp.sum(grad_mixed.astype(F32), axis=1),
        jnp.sum(grad_hidden_two * normed_two, axis=1),
        jnp.sum(grad_hidden_two, axis=1),
        jnp.sum(grad_out, axis=1),
        jnp.sum(grad_pre.astype(F32), axis=1),
    ]
    grad_send, *middle_sums = lax.optimization_barrier(
        [to_heads(grad_attended, ctx, lanes)] + middle_sums
    )
    grad_slots = exchange(grad_send)

    def plane_rows(data, later):
        side = after(to_side(data), *later)
        return data, side, to_core(jnp.concatenate([data, side], axis=-1))

    def all_rows(own, side, core):
        size = own.shape[-1]
        return jnp.concatenate([own, core[..., :size], side, core[..., size:]], axis=-1)

    def plane_units(units, later):
        size = units.shape[0] // (planes // 2 * 4)
        grid = units.reshape(planes // 2, 2, 2, size, units.shape[1])
        kept, sent = split(grid, my_core, 2)
        both = jnp.concatenate([kept, after(to_core(sent), *later)], axis=-1)
        kept, sent = split(both, my_side, 1)
        return kept, to_side(sent)

    def all_units(kept, got):
        return jnp.concatenate([kept, got], axis=-1).reshape(-1, 2 * kept.shape[-1])

    def flat(units):
        return units.reshape(-1, units.shape[-1])

    def line_sum(parts):
        return lax.psum_scatter(
            parts, "ctx", scatter_dimension=0, axis_index_groups=lines, tiled=False
        )

    active_kept, active_got = plane_units(activated, (grad_two,))
    pre_kept, pre_got = plane_units(grad_pre, (two_send,))
    out_grad_early = jnp.concatenate([own_out_grad, after(other_out_grad, qkv_heads)], axis=1)
    out_grad_all = plane_rows(out_grad_early, (two_send,))

    down_parts = tokens_product((flat(active_kept), flat(after(active_got, two_send))), out_grad_all)
    down_parts = down_parts.reshape(planes, -1, down_parts.shape[2])
    hidden_two_all = plane_rows(hidden_two_pair, (two_send,))
    up_parts = tokens_product((flat(pre_kept), flat(after(pre_got, down_parts))), hidden_two_all)
    up_kept, up_sent = [x[0] for x in split(up_parts, my_dp, 0)]
    up_got = across(up_sent)

    line_ready = after(down_parts, hidden_one_all)
    down_sums = line_sum(line_ready)[:, :half_cols]
    owner = [
        (d * ctx + (e * planes // 2 + z) * 4 + q, e * ctx + (d * planes // 2 + z) * 4 + q)
        for d in range(2)
        for e in range(2)
        for z in range(planes // 2)
        for q in range(4)
    ]

    proj_slots = attend_backward(
        natural,
        out_rows,
        log_rows,
        after(grad_slots, line_ready),
        block_order,
        head_width,
        score_scale,
    )
    proj_back = exchange(proj_slots)
    grad_proj = jnp.concatenate(
        [from_heads(proj_back[:, kind], width) for kind in range(3)], axis=0
    )
    down_grad = lax.ppermute(after(down_sums, proj_slots), ("dp", "ctx"), owner).astype(F32)

    attended_late = after(attended, hidden_two)
    attended_got = after(across(attended_late), proj_slots)
    attended_pair = jnp.concatenate([attended_late, attended_got], axis=1)
    size = width // ctx
    grid = attended_pair.reshape(planes, 2, 2, size, 2 * tokens)
    kept, sent = split(grid, my_core, 2)
    both = jnp.concatenate([kept, to_core(sent)], axis=-1)
    kept, sent = split(both, my_side, 1)
    out_units = (kept, after(to_side(sent), proj_slots))
    mixed_pair = jnp.concatenate([mixed_own, after(across(mixed_other), grad_send)], axis=1)
    mixed_all = all_rows(*plane_rows(mixed_pair, (proj_slots,)))
    out_part = dot32(all_units(*out_units), mixed_all, "ct,dt->cd").astype(BF16)
    out_part = out_part.reshape(planes, size, half_cols)
    unit_block = 2 * half_units // ctx
    up_parts = joined(my_dp, up_kept, after(up_got, proj_slots))
    up_parts = up_parts.reshape(planes, unit_block, -1)
    up_sums = line_sum(up_parts)
    out_sums = line_sum(after(out_part, up_parts))

    proj_mine, proj_rest = split(grad_proj, my_dp, 0)
    proj_pair = jnp.concatenate([proj_mine, across(proj_rest)], axis=1)
    grad_one = dot32(w_qkv, proj_pair, "de,et->dt")
    one_send = grad_one[:, tokens:].astype(BF16)
    grad_one_got = across(one_send)
    grad_hidden_one = grad_one[:, :tokens] + grad_one_got.astype(F32)
    input_grad = grad_residual + norm_back(grad_hidden_one * gain_one, normed_one, inverse_one)
    input_grad = input_grad.astype(BF16).T

    qkv_part = dot32(
        proj_slots, hidden_one_all.reshape(ctx, tokens, width), "sklt,std->kld"
    )
    qkv_kept, qkv_send = split(qkv_part, my_dp, 2)
    qkv_send = qkv_send.astype(BF16)
    qkv_sums = qkv_kept + across(qkv_send).astype(F32)
    qkv_sums = qkv_sums.astype(BF16)
    block = 2 * half_proj // ctx
    edges = []
    for source in range(ctx):
        for kind in range(3):
            first = kind * width + source * lanes
            last = min(first + lanes, (kind + 1) * width)
            if first < last:
                for target in range(first // block, (last - 1) // block + 1):
                    edges.append((source, target, kind))
    rounds = rounds_of(edges)
    kinds = [[0] * ctx for _ in rounds]
    offsets = [[-lanes] * ctx for _ in rounds]
    for number, edges_now in enumerate(rounds):
        for source, target, kind in edges_now:
            kinds[number][source] = kind
            offsets[number][target] = kind * width + source * lanes - target * block
    mine = jnp.arange(ctx, dtype=jnp.int32)[None, :] == my_ctx
    kinds = jnp.sum(jnp.where(mine, jnp.asarray(kinds, jnp.int32), 0), axis=1)[:, None, None]
    offsets = jnp.sum(jnp.where(mine, jnp.asarray(offsets, jnp.int32), 0), axis=1)
    place = offsets[:, None] + jnp.arange(lanes, dtype=jnp.int32)[None, :]
    targets = jnp.arange(block, dtype=jnp.int32)[:, None]
    chosen = (targets == place.reshape(1, -1)).astype(BF16)
    pieces = jnp.where(kinds == 0, qkv_sums[:1], jnp.where(kinds == 1, qkv_sums[1:2], qkv_sums[2:]))
    received = []
    for number, edges_now in enumerate(rounds):
        piece = lax.ppermute(pieces[number], "ctx", [edge[:2] for edge in edges_now])
        received.append(after(piece, grad_one_got))
    received = jnp.concatenate(received, axis=0)
    qkv_grad = dot32(chosen, received, "cr,rd->cd").T

    activated_late = after(activated, grad_one_got)
    down_sum = joined(
        my_dp,
        dot32(activated_late, down_rows, "ft,fd->dt"),
        joined(
            my_core,
            dot32(activated_late, down_mine, "ft,fd->dt"),
            dot32(activated_late, down_rest, "ft,fd->dt"),
        ),
    )
    down_got = across(down_sum[:, tokens:].astype(BF16))
    layer_out = residual + (down_sum[:, :tokens] + down_got.astype(F32)) + column(down_bias)
    layer_out = layer_out.astype(BF16).T

    def at_dp(vector):
        none = jnp.zeros_like(vector)
        return joined(my_dp, vector, none)

    devices = 2 * ctx

    def everywhere(packed):
        return lax.all_to_all(packed, ("dp", "ctx"), 0, 0, tiled=True)

    def pieces_of(totals, items):
        first = 0
        for item in items:
            yield totals[first : first + item.shape[0]]
            first += item.shape[0]

    early = middle_sums[:4] + [at_dp(middle_sums[4])]
    packed = after(jnp.concatenate(early), grad_slots)
    size = -(-packed.shape[0] // (devices * 128)) * 128
    packed = jnp.pad(packed, (0, devices * size - packed.shape[0]))
    mine = everywhere(packed.reshape(devices, size // 128, 128))
    mine = jnp.sum(mine, axis=0).reshape(-1)
    head_sums = jnp.sum(proj_slots.astype(F32), axis=(0, 3))
    packed = jnp.concatenate([mine, head_sums[0], head_sums[2]])
    packed = jnp.pad(packed, (0, -packed.shape[0] % 128)).reshape(1, -1, 128)
    packed = jnp.broadcast_to(packed, (devices,) + packed.shape[1:])
    totals = after(everywhere(packed), grad_one_got).reshape(devices, -1)
    pieces = list(pieces_of(totals[:, :size].reshape(-1), early))
    head_sums = totals[:, size : size + 2 * lanes].reshape(2, ctx, 2, lanes)
    head_sums = jnp.transpose(jnp.sum(head_sums, axis=0), (1, 0, 2)).reshape(2, -1)[:, :width]
    late = [jnp.sum(grad_hidden_one * normed_one, axis=1), jnp.sum(grad_hidden_one, axis=1)]
    packed = jnp.concatenate(late).reshape(1, -1, 128)
    packed = jnp.broadcast_to(packed, (devices,) + packed.shape[1:])
    totals = jnp.sum(everywhere(packed), axis=0)
    ln1 = list(pieces_of(totals.reshape(-1), late))
    up_grad = after(up_sums, totals)[:, :half_cols].astype(F32).T
    out_weight_grad = after(out_sums, totals).astype(F32)

    return (
        layer_out.reshape(layer_in.shape),
        input_grad.reshape(layer_in.shape),
        ln1[0],
        ln1[1],
        qkv_grad,
        head_sums,
        out_weight_grad,
        pieces[0],
        pieces[1],
        pieces[2],
        up_grad,
        pieces[4],
        down_grad,
        pieces[3],
    )


def layer(ctx, *arrays):
    return shards(ctx, *arrays)


def solution(mesh):
    placed = (
        P("dp", "ctx", None),
        P("dp", "ctx", None),
        P("dp", None),
        P(),
        P(),
        P(None, "dp"),
        P(),
        P(None, "dp"),
        P(),
        P(),
        P(),
        P(None, "dp"),
        P(),
        P(None, "dp"),
        P(),
    )
    return jax.shard_map(
        partial(layer, mesh.shape["ctx"]),
        mesh=mesh,
        in_specs=placed,
        out_specs=(
            P("dp", "ctx", None),
            P("dp", "ctx", None),
            P(),
            P(),
            P("dp", "ctx"),
            P(),
            P("ctx", "dp"),
            P(),
            P(),
            P(),
            P("dp", "ctx"),
            P(),
            P("ctx", "dp"),
            P(),
        ),
        check_vma=False,
    )
```

```python
from functools import partial
import math

import jax
import jax.numpy as jnp
from jax import lax
from jax.experimental import pallas as pl
from jax.experimental.pallas import tpu as pltpu
from jax.sharding import PartitionSpec as P

from jax.experimental.layout import Layout, with_layout_constraint

HEADS = 25


EPS = 1e-05
GELU_C = 0.7978845608028654
NEG_FILL = -1e30
BF16 = jnp.bfloat16
F32 = jnp.float32


def normalize(data):
    centre = jnp.mean(data, axis=0, keepdims=True)
    shifted = data - centre
    inverse = lax.rsqrt(jnp.mean(shifted * shifted, axis=0, keepdims=True) + EPS)
    return (shifted * inverse, inverse)


def norm_back(grad_hat, normed, inverse):
    first_mean = jnp.mean(grad_hat, axis=0, keepdims=True)
    second = jnp.mean(grad_hat * normed, axis=0, keepdims=True)
    return inverse * (grad_hat - first_mean - normed * second)


def gelu_parts(values):
    cubic_term = 0.044715 * values * values * values
    tangent = jnp.tanh(GELU_C * (values + cubic_term))
    output = 0.5 * values * (1.0 + tangent)
    gelu_slope = 0.5 * (1.0 + tangent) + 0.5 * values * (1.0 - tangent * tangent) * GELU_C * (
        1.0 + 3.0 * 0.044715 * values * values
    )
    return (output, gelu_slope)


def head_parts(value, head_width):
    heads = value.shape[1] // head_width
    if heads == 1:
        return [value]
    lane = lax.broadcasted_iota(jnp.int32, value.shape, 1) // head_width
    return [jnp.where(lane == h, value, jnp.zeros_like(value)) for h in range(heads)]


def by_head(columns, shape, head_width):
    if len(columns) == 1:
        return jnp.broadcast_to(columns[0], shape)
    lane = lax.broadcasted_iota(jnp.int32, shape, 1) // head_width
    result = jnp.broadcast_to(columns[-1], shape)
    for h in range(len(columns) - 2, -1, -1):
        result = jnp.where(lane == h, columns[h], result)
    return result


def dot(a, b, contract):
    return lax.dot_general(a, b, (contract, ((), ())), preferred_element_type=F32)


def each_query_block(length, block, visit):
    if length // block <= 4:
        for index in range(length // block):
            chunks = [(0, index * block, False)] if index else []
            visit(index * block, chunks + [(index * block, block, True)])
    else:

        def step(index, carry):
            visit(pl.multiple_of(index * block, block), [(0, length, True)])
            return carry

        lax.fori_loop(0, length // block, step, 0)


def visible_mask(first_row, rows, first_key, keys):
    row_ids = first_row + lax.broadcasted_iota(jnp.int32, (rows, keys), 0)
    key_ids = first_key + lax.broadcasted_iota(jnp.int32, (rows, keys), 1)
    return key_ids <= row_ids


def slot_rows(order, seq, source, half):
    return [pl.multiple_of(order[seq, 2 * source + part] * half, half) for part in range(2)]


def forward_kernel(
    half, block, head_width, score_scale, order, qkv, slot_out, natural, out_rows, log_rows
):
    sources = qkv.shape[0]
    kinds, seqs, length, lanes = natural.shape

    def place(source, carry):
        for kind in range(kinds):
            rows = qkv[source, kind].T
            for seq in range(seqs):
                for part, first in enumerate(slot_rows(order, seq, source, half)):
                    begin = (2 * seq + part) * half
                    natural[kind, seq, pl.ds(first, half), :] = rows[begin : begin + half, :]
        return carry

    lax.fori_loop(0, sources, place, 0)

    def visit(seq, first_row, chunks):
        rows = pl.ds(first_row, block)
        queries = natural[0, seq, rows, :] * jnp.asarray(score_scale, BF16)
        outputs = []
        logs = []
        for query in head_parts(queries, head_width):
            scores = []
            for first_key, keys, masked in chunks:
                part = dot(query, natural[1, seq, first_key : first_key + keys, :], ((1,), (1,)))
                if masked:
                    part = jnp.where(
                        visible_mask(first_row, block, first_key, keys), part, NEG_FILL
                    )
                scores.append(part)
            top = jnp.max(scores[0], axis=1, keepdims=True)
            for part in scores[1:]:
                top = jnp.maximum(top, jnp.max(part, axis=1, keepdims=True))
            total = jnp.zeros((block, 1), F32)
            summed = jnp.zeros((block, lanes), F32)
            for (first_key, keys, masked), part in zip(chunks, scores):
                weights = jnp.exp(part - top)
                total = total + jnp.sum(weights, axis=1, keepdims=True)
                coarse = weights.astype(BF16)
                fine = (weights - coarse.astype(F32)).astype(BF16)
                values = natural[2, seq, first_key : first_key + keys, :]
                summed = summed + dot(coarse, values, ((1,), (0,))) + dot(fine, values, ((1,), (0,)))
            outputs.append(summed / total)
            logs.append(top + jnp.log(total))
        result = outputs[0]
        if len(outputs) > 1:
            lane = lax.broadcasted_iota(jnp.int32, result.shape, 1) // head_width
            for h in range(1, len(outputs)):
                result = jnp.where(lane == h, outputs[h], result)
        out_rows[seq, rows, :] = result.astype(BF16)
        log_rows[seq, rows, :] = by_head(logs, result.shape, head_width)

    def one_sequence(seq, carry):
        each_query_block(length, block, partial(visit, seq))
        return carry

    lax.fori_loop(0, seqs, one_sequence, 0)

    def give(source, carry):
        rows = [
            out_rows[seq, pl.ds(first, half), :]
            for seq in range(seqs)
            for first in slot_rows(order, seq, source, half)
        ]
        slot_out[source] = jnp.concatenate(rows, axis=0).T
        return carry

    lax.fori_loop(0, sources, give, 0)


def backward_kernel(
    half,
    block,
    head_width,
    score_scale,
    order,
    natural,
    out_rows,
    log_rows,
    grad_slots,
    slot_out,
    grad_rows,
    grad_natural,
):
    sources = grad_slots.shape[0]
    kinds, seqs, length, lanes = natural.shape

    def place(source, carry):
        rows = grad_slots[source].T
        for seq in range(seqs):
            for part, first in enumerate(slot_rows(order, seq, source, half)):
                begin = (2 * seq + part) * half
                grad_rows[seq, pl.ds(first, half), :] = rows[begin : begin + half, :]
        return carry

    lax.fori_loop(0, sources, place, 0)
    grad_natural[1:] = jnp.zeros((kinds - 1, seqs, length, lanes), F32)

    def visit(seq, first_row, chunks):
        rows = pl.ds(first_row, block)
        queries = natural[0, seq, rows, :] * jnp.asarray(score_scale, BF16)
        grads = grad_rows[seq, rows, :]
        products = grads.astype(F32) * out_rows[seq, rows, :].astype(F32)
        logs = log_rows[seq, rows, :]
        query_sum = jnp.zeros(products.shape, F32)
        parts = zip(
            head_parts(queries, head_width),
            head_parts(grads, head_width),
            head_parts(products, head_width),
        )
        for h, (query, grad, product) in enumerate(parts):
            delta = jnp.sum(product, axis=1, keepdims=True)
            log_total = logs[:, h * head_width : h * head_width + 1]
            for first_key, keys, masked in chunks:
                span = slice(first_key, first_key + keys)
                key_block = natural[1, seq, span, :]
                scores = dot(query, key_block, ((1,), (1,)))
                probs = jnp.exp(scores - log_total)
                if masked:
                    probs = jnp.where(
                        visible_mask(first_row, block, first_key, keys), probs, 0.0
                    )
                grad_probs = dot(grad, natural[2, seq, span, :], ((1,), (1,)))
                grad_scores = (probs * (grad_probs - delta)).astype(BF16)
                grad_natural[2, seq, span, :] += dot(probs.astype(BF16), grad, ((0,), (0,)))
                grad_natural[1, seq, span, :] += dot(grad_scores, query, ((0,), (0,)))
                query_sum = query_sum + dot(
                    grad_scores, head_parts(key_block, head_width)[h], ((1,), (0,))
                )
        grad_natural[0, seq, rows, :] = query_sum * score_scale

    def one_sequence(seq, carry):
        each_query_block(length, block, partial(visit, seq))
        return carry

    lax.fori_loop(0, seqs, one_sequence, 0)

    def give(source, carry):
        for kind in range(kinds):
            rows = [
                grad_natural[kind, seq, pl.ds(first, half), :]
                for seq in range(seqs)
                for first in slot_rows(order, seq, source, half)
            ]
            slot_out[source, kind] = jnp.concatenate(rows, axis=0).astype(BF16).T
        return carry

    lax.fori_loop(0, sources, give, 0)


def in_vmem(count):
    return [pl.BlockSpec(memory_space=pltpu.VMEM)] * count


def attend_forward(qkv, order, head_width, score_scale):
    sources, kinds, lanes, tokens = qkv.shape
    seqs = order.shape[0]
    length = sources * tokens // seqs
    block = math.gcd(length, 256)
    return pl.pallas_call(
        partial(forward_kernel, tokens // seqs // 2, block, head_width, score_scale),
        in_specs=[pl.BlockSpec(memory_space=pltpu.SMEM)] + in_vmem(1),
        out_specs=in_vmem(4),
        out_shape=[
            jax.ShapeDtypeStruct((sources, lanes, tokens), BF16),
            jax.ShapeDtypeStruct((kinds, seqs, length, lanes), BF16),
            jax.ShapeDtypeStruct((seqs, length, lanes), BF16),
            jax.ShapeDtypeStruct((seqs, length, lanes), F32),
        ],
        name="attf",
    )(order, qkv)


def attend_backward(natural, out_rows, log_rows, grad_slots, order, head_width, score_scale):
    sources, lanes, tokens = grad_slots.shape
    kinds, seqs, length, lanes = natural.shape
    block = math.gcd(length, 256)
    return pl.pallas_call(
        partial(backward_kernel, tokens // seqs // 2, block, head_width, score_scale),
        in_specs=[pl.BlockSpec(memory_space=pltpu.SMEM)] + in_vmem(4),
        out_specs=in_vmem(1)[0],
        scratch_shapes=[
            pltpu.VMEM((seqs, length, lanes), BF16),
            pltpu.VMEM((kinds, seqs, length, lanes), F32),
        ],
        out_shape=jax.ShapeDtypeStruct((sources, kinds, lanes, tokens), BF16),
        name="attb",
    )(order, natural, out_rows, log_rows, grad_slots)


def product_kernel(flip, kept, got, own, side, core, parts):
    units, tokens = kept.shape[0], own.shape[1]
    halves, _, width = parts.shape
    block = own.shape[0] // halves
    pairs = (
        (kept, 0, own, 0),
        (kept, tokens, core, 0),
        (got, 0, side, 0),
        (got, tokens, core, tokens),
    )
    step = units // 2

    def one_half(half, carry):
        for first in range(0, units, step):
            total = jnp.zeros((step, block), F32)
            for left, left_at, right, right_at in pairs:
                a = left[first : first + step, left_at : left_at + tokens]
                rows = pl.ds(pl.multiple_of((half ^ flip[0]) * block, 16), block)
                b = right[rows, right_at : right_at + tokens]
                total = total + dot(a, b, ((1,), (1,)))
            parts[half, first : first + step, :block] = total.astype(BF16)
            if width > block:
                blank = jnp.zeros((step, width - block), BF16)
                parts[half, first : first + step, block:] = blank
        return carry

    lax.fori_loop(0, halves, one_half, 0)


def tokens_product(units, rows, flip):
    kept, got = units
    own, side, core = rows
    width = own.shape[0] // 2
    return pl.pallas_call(
        product_kernel,
        in_specs=[pl.BlockSpec(memory_space=pltpu.SMEM)] + in_vmem(5),
        out_specs=in_vmem(1)[0],
        out_shape=jax.ShapeDtypeStruct((2, kept.shape[0], width + -width % 128), BF16),
        name="prod",
    )(jnp.full((1,), flip, jnp.int32), kept, got, own, side, core)


def rounds_of(edges):
    at_source, at_target = {}, {}
    for source, target, item in edges:
        sends, gets = at_source.setdefault(source, {}), at_target.setdefault(target, {})
        first = next(r for r in range(len(edges)) if r not in sends)
        last = next(r for r in range(len(edges)) if r not in gets)
        if first != last:
            path, node, side, look = [], target, at_target, first
            while look in side.setdefault(node, {}):
                edge = side[node][look]
                path.append((edge, look))
                node = edge[0] if side is at_target else edge[1]
                side = at_source if side is at_target else at_target
                look = first + last - look
            for edge, was in path:
                del at_source[edge[0]][was], at_target[edge[1]][was]
            for edge, was in path:
                now = first + last - was
                at_source[edge[0]][now] = at_target[edge[1]][now] = edge
        sends[first] = gets[first] = (source, target, item)
    count = 1 + max(r for sends in at_source.values() for r in sends)
    return [[sends[r] for sends in at_source.values() if r in sends] for r in range(count)]


def to_heads(data, devices, lanes):
    width, tokens = data.shape
    return jnp.pad(data, ((0, devices * lanes - width), (0, 0))).reshape(devices, lanes, tokens)


def from_heads(blocks, width):
    devices, lanes, tokens = blocks.shape
    return blocks.reshape(devices * lanes, tokens)[:width]


def shards(
    ctx,
    layer_in,
    out_grad,
    block_order,
    ln1_gain,
    ln1_bias,
    w_qkv,
    qv_bias,
    w_out,
    out_bias,
    ln2_gain,
    ln2_bias,
    w_up,
    up_bias,
    w_down,
    down_bias,
):
    seqs, tok_rows, width = layer_in.shape
    tokens = seqs * tok_rows
    head_width = width // HEADS
    score_scale = 1.0 / math.sqrt(head_width)
    lanes = -(-HEADS // ctx) * head_width
    half_units = w_up.shape[1]
    half_cols = w_out.shape[1]
    half_proj = w_qkv.shape[1]
    planes = ctx // 4
    my_dp = lax.axis_index("dp")
    my_ctx = lax.axis_index("ctx")
    my_core = my_ctx % 2
    my_side = (my_ctx // 2) % 2
    core_swap = [(i, i ^ 1) for i in range(ctx)]
    side_swap = [(i, i ^ 2) for i in range(ctx)]
    lines = [[q + 4 * z for z in range(planes)] for q in range(4)]

    def across(x):
        return lax.ppermute(x, "dp", [(0, 1), (1, 0)])

    def to_core(x):
        return lax.ppermute(x, "ctx", core_swap)

    def to_side(x):
        return lax.ppermute(x, "ctx", side_swap)

    def exchange(x):
        return lax.all_to_all(x, "ctx", 0, 0, tiled=True)

    def after(x, *earlier):
        return lax.optimization_barrier((x,) + earlier)[0]

    def pick(x, index, axis, count=2):
        size = x.shape[axis] // count
        return lax.dynamic_slice_in_dim(x, index * size, size, axis)

    def split(x, index, axis):
        return pick(x, index, axis), pick(x, 1 - index, axis)

    def joined(index, mine, other, axis=0):
        return jnp.where(
            index == 0,
            jnp.concatenate([mine, other], axis=axis),
            jnp.concatenate([other, mine], axis=axis),
        )

    def dot32(a, b, spec):
        return jnp.einsum(spec, a, b, preferred_element_type=F32)

    column = lambda vector: vector[:, None]

    own_in = layer_in.reshape(tokens, width).T
    own_out_grad = out_grad.reshape(tokens, width).T
    other_in = across(own_in)
    stream = own_in.astype(F32)
    normed_one, inverse_one = normalize(stream)
    gain_one, bias_one = column(ln1_gain), column(ln1_bias)
    hidden_one = (normed_one * gain_one + bias_one).astype(BF16)
    hidden_one_other = (normalize(other_in.astype(F32))[0] * gain_one + bias_one).astype(BF16)
    proj_bias = jnp.concatenate([qv_bias[0], jnp.zeros_like(qv_bias[0]), qv_bias[1]])
    proj_bias = column(pick(proj_bias, my_dp, 0))
    proj_other = (dot32(w_qkv, hidden_one_other, "de,dt->et") + proj_bias).astype(BF16)
    proj_got = across(proj_other)
    proj_own = (dot32(w_qkv, hidden_one, "de,dt->et") + proj_bias).astype(BF16)
    proj_own = lax.optimization_barrier(proj_own)
    low = jnp.where(my_dp == 0, proj_own, proj_got)
    high = jnp.where(my_dp == 0, proj_got, proj_own)
    queries = low[:width]
    keys = jnp.concatenate([low[width:], high[: 2 * width - half_proj]], axis=0)
    values = high[2 * width - half_proj :]
    send = jnp.stack([to_heads(x, ctx, lanes) for x in (queries, keys, values)], axis=1)
    qkv_heads = exchange(send)

    out_mine = across(after(pick(w_out, my_core, 0), proj_got))
    other_out_grad = across(after(own_out_grad, proj_got))
    down_rows = pick(w_down, my_dp, 0)
    down_send = pick(pick(w_down, 1 - my_dp, 0), my_core, 1)
    down_mine = across(after(down_send, proj_got))
    out_rest = to_core(after(out_mine, qkv_heads))

    hidden_one_all = lax.all_gather(after(hidden_one.T, qkv_heads), "ctx", axis=0, tiled=True)

    attended_slots, natural, out_rows, log_rows = attend_forward(
        qkv_heads, block_order, head_width, score_scale
    )
    attended = from_heads(exchange(attended_slots), width)
    down_rest = to_core(after(down_mine, attended))

    attended_mine, attended_rest = split(attended, my_core, 0)
    mixed = joined(
        my_dp,
        dot32(w_out, attended, "ab,at->bt"),
        dot32(out_mine, attended_mine, "ab,at->bt") + dot32(out_rest, attended_rest, "ab,at->bt"),
    )
    residual = stream + mixed + column(out_bias)
    normed_two, inverse_two = normalize(residual)
    gain_two = column(ln2_gain)
    hidden_two = (normed_two * gain_two + column(ln2_bias)).astype(BF16)
    hidden_two_pair = jnp.concatenate([hidden_two, across(hidden_two)], axis=1)

    out_grad_pair = after(
        jnp.concatenate([own_out_grad, after(other_out_grad, attended)], axis=1), hidden_two
    )
    out_grad_own, out_grad_rest = split(out_grad_pair, my_dp, 0)
    rest_mine, rest_rest = split(out_grad_rest, my_core, 0)
    grad_active = (
        dot32(down_rows, out_grad_own, "fd,dt->ft")
        + dot32(down_mine, rest_mine, "fd,dt->ft")
        + dot32(down_rest, rest_rest, "fd,dt->ft")
    )
    pre_act = dot32(w_up, hidden_two_pair, "df,dt->ft") + column(pick(up_bias, my_dp, 0))
    activated_wide, gelu_slope = gelu_parts(pre_act)
    activated = with_layout_constraint(activated_wide.astype(BF16), Layout((0, 1)))
    grad_pre = with_layout_constraint((grad_active * gelu_slope).astype(BF16), Layout((0, 1)))
    grad_two = dot32(grad_pre, w_up, "ft,df->dt")
    two_send = grad_two[:, tokens:].astype(BF16)
    grad_two_got = across(two_send)
    grad_hidden_two = grad_two[:, :tokens] + grad_two_got.astype(F32)

    grad_out = own_out_grad.astype(F32)
    grad_residual = grad_out + norm_back(grad_hidden_two * gain_two, normed_two, inverse_two)
    grad_mixed = grad_residual.astype(BF16)
    mixed_own, mixed_other = split(grad_mixed, my_dp, 0)
    grad_attended = (
        dot32(w_out, mixed_own, "ab,bt->at")
        + joined(
            my_core,
            dot32(out_mine, mixed_other, "ab,bt->at"),
            dot32(out_rest, mixed_other, "ab,bt->at"),
        )
    ).astype(BF16)
    middle_sums = [
        jnp.sum(grad_mixed.astype(F32), axis=1),
        jnp.sum(grad_hidden_two * normed_two, axis=1),
        jnp.sum(grad_hidden_two, axis=1),
        jnp.sum(grad_out, axis=1),
        jnp.sum(grad_pre.astype(F32), axis=1),
    ]
    grad_send, *middle_sums = lax.optimization_barrier(
        [to_heads(grad_attended, ctx, lanes)] + middle_sums
    )
    grad_slots = exchange(grad_send)

    def plane_rows(data, later):
        side = after(to_side(data), *later)
        return data, side, to_core(jnp.concatenate([data, side], axis=-1))

    def plane_units(units, later):
        size = units.shape[0] // (planes // 2 * 4)
        grid = units.reshape(planes // 2, 2, 2, size, units.shape[1])
        kept, sent = split(grid, my_core, 2)
        both = jnp.concatenate([kept, after(to_core(sent), *later)], axis=-1)
        kept, sent = split(both, my_side, 1)
        return kept, to_side(sent)

    def flat(units):
        return units.reshape(-1, units.shape[-1])

    def line_sum(parts):
        return lax.psum_scatter(
            parts, "ctx", scatter_dimension=0, axis_index_groups=lines, tiled=False
        )

    active_kept, active_got = plane_units(activated, (grad_two,))
    pre_kept, pre_got = plane_units(grad_pre, (two_send,))
    out_grad_early = jnp.concatenate([own_out_grad, after(other_out_grad, qkv_heads)], axis=1)
    out_grad_all = plane_rows(out_grad_early, (two_send,))

    units = (flat(active_kept), flat(after(active_got, two_send)))
    down_parts = tokens_product(units, out_grad_all, 0)
    down_parts = down_parts.reshape(planes, -1, down_parts.shape[2])
    hidden_two_all = plane_rows(hidden_two_pair, (two_send,))
    units = (flat(pre_kept), flat(after(pre_got, down_parts)))
    up_kept, up_sent = tokens_product(units, hidden_two_all, my_dp)
    up_got = across(up_sent)

    line_ready = after(down_parts, hidden_one_all)
    down_sums = line_sum(line_ready)[:, :half_cols]
    owner = [
        (d * ctx + (e * planes // 2 + z) * 4 + q, e * ctx + (d * planes // 2 + z) * 4 + q)
        for d in range(2)
        for e in range(2)
        for z in range(planes // 2)
        for q in range(4)
    ]

    proj_slots = attend_backward(
        natural,
        out_rows,
        log_rows,
        after(grad_slots, line_ready),
        block_order,
        head_width,
        score_scale,
    )
    proj_back = exchange(proj_slots)
    grad_proj = jnp.concatenate(
        [from_heads(proj_back[:, kind], width) for kind in range(3)], axis=0
    )
    down_grad = lax.ppermute(after(down_sums, proj_slots), ("dp", "ctx"), owner)

    unit_block = 2 * half_units // ctx
    up_parts = joined(my_dp, up_kept, after(up_got, proj_slots))
    up_parts = up_parts.reshape(planes, unit_block, -1)
    up_sums = line_sum(up_parts)
    proj_mine, proj_rest = split(grad_proj, my_dp, 0)
    proj_pair = jnp.concatenate([proj_mine, across(proj_rest)], axis=1)
    grad_one = dot32(w_qkv, proj_pair, "de,et->dt")
    one_send = grad_one[:, tokens:].astype(BF16)
    grad_one_got = across(one_send)
    grad_hidden_one = grad_one[:, :tokens] + grad_one_got.astype(F32)
    input_grad = grad_residual + norm_back(grad_hidden_one * gain_one, normed_one, inverse_one)
    input_grad = input_grad.astype(BF16).T

    attended_late = after(attended, hidden_two)
    attended_got = after(across(attended_late), proj_back)
    attended_pair = jnp.concatenate([attended_late, attended_got], axis=1)
    size = width // ctx
    grid = attended_pair.reshape(planes, 2, 2, size, 2 * tokens)
    kept, sent = split(grid, my_core, 2)
    both = jnp.concatenate([kept, to_core(sent)], axis=-1)
    kept, sent = split(both, my_side, 1)
    out_units = (kept, after(to_side(sent), proj_slots))
    mixed_pair = jnp.concatenate([mixed_own, after(across(mixed_other), proj_back)], axis=1)
    mixed_all = plane_rows(mixed_pair, (one_send,))
    out_part = 0.0
    step = 2 * tokens
    kept, got = [flat(units) for units in out_units]
    for units, at, rows in ((kept, 0, 0), (kept, 1, 2), (got, 0, 1), (got, 1, 2)):
        begin = step if rows == 2 and units is got else 0
        rows = mixed_all[rows][:, begin : begin + step]
        out_part += dot32(units[:, at * step : (at + 1) * step], rows, "ct,dt->cd")
    out_part = out_part.astype(BF16)
    out_part = out_part.reshape(planes, size, half_cols)
    out_part = jnp.pad(out_part, ((0, 0), (0, -size % 8), (0, -half_cols % 128)))
    out_sums = line_sum(after(out_part, up_parts))[:size, :half_cols]

    qkv_part = dot32(
        proj_slots, hidden_one_all.reshape(ctx, tokens, width), "sklt,std->kld"
    )
    qkv_kept, qkv_send = split(qkv_part, my_dp, 2)
    qkv_send = qkv_send.astype(BF16)
    qkv_sums = qkv_kept + across(qkv_send).astype(F32)
    qkv_sums = qkv_sums.astype(BF16)
    block = 2 * half_proj // ctx
    edges = []
    for source in range(ctx):
        for kind in range(3):
            first = kind * width + source * lanes
            last = min(first + lanes, (kind + 1) * width)
            if first < last:
                for target in range(first // block, (last - 1) // block + 1):
                    edges.append((source, target, kind))
    rounds = rounds_of(edges)
    kinds = [[0] * ctx for _ in rounds]
    offsets = [[-lanes] * ctx for _ in rounds]
    for number, edges_now in enumerate(rounds):
        for source, target, kind in edges_now:
            kinds[number][source] = kind
            offsets[number][target] = kind * width + source * lanes - target * block
    mine = jnp.arange(ctx, dtype=jnp.int32)[None, :] == my_ctx
    kinds = jnp.sum(jnp.where(mine, jnp.asarray(kinds, jnp.int32), 0), axis=1)[:, None, None]
    offsets = jnp.sum(jnp.where(mine, jnp.asarray(offsets, jnp.int32), 0), axis=1)
    place = offsets[:, None] + jnp.arange(lanes, dtype=jnp.int32)[None, :]
    targets = jnp.arange(block, dtype=jnp.int32)[:, None]
    chosen = (targets == place.reshape(1, -1)).astype(BF16)
    pieces = jnp.where(kinds == 0, qkv_sums[:1], jnp.where(kinds == 1, qkv_sums[1:2], qkv_sums[2:]))
    received = []
    for number, edges_now in enumerate(rounds):
        piece = lax.ppermute(pieces[number], "ctx", [edge[:2] for edge in edges_now])
        received.append(piece)

    activated_late = after(activated, grad_one_got)
    down_sum = joined(
        my_dp,
        dot32(activated_late, down_rows, "ft,fd->dt"),
        joined(
            my_core,
            dot32(activated_late, down_mine, "ft,fd->dt"),
            dot32(activated_late, down_rest, "ft,fd->dt"),
        ),
    )
    down_got = across(down_sum[:, tokens:].astype(BF16))
    layer_out = residual + (down_sum[:, :tokens] + down_got.astype(F32)) + column(down_bias)
    layer_out = layer_out.astype(BF16).T

    def at_dp(vector):
        none = jnp.zeros_like(vector)
        return joined(my_dp, vector, none)

    devices = 2 * ctx

    def everywhere(packed):
        return lax.all_to_all(packed, ("dp", "ctx"), 0, 0, tiled=True)

    def pieces_of(totals, items):
        first = 0
        for item in items:
            yield totals[first : first + item.shape[0]]
            first += item.shape[0]

    early = middle_sums[:4] + [at_dp(middle_sums[4])]
    packed = after(jnp.concatenate(early), proj_back)
    size = -(-packed.shape[0] // (devices * 128)) * 128
    packed = jnp.pad(packed, (0, devices * size - packed.shape[0]))
    mine = everywhere(packed.reshape(devices, size // 128, 128))
    mine = jnp.sum(after(mine, grad_one_got), axis=0).reshape(-1)
    head_sums = jnp.sum(proj_slots.astype(F32), axis=(0, 3))
    late = [jnp.sum(grad_hidden_one * normed_one, axis=1), jnp.sum(grad_hidden_one, axis=1)]
    packed = jnp.concatenate([mine, head_sums[0], head_sums[2]] + late)
    packed = jnp.pad(packed, (0, -packed.shape[0] % 128)).reshape(1, -1, 128)
    packed = jnp.broadcast_to(packed, (devices,) + packed.shape[1:])
    totals = everywhere(packed).reshape(devices, -1)
    pieces_in = [after(piece, packed) for piece in received]
    qkv_grad = sum(
        dot32(chosen[:, i * lanes : (i + 1) * lanes], piece, "cr,rd->cd")
        for i, piece in enumerate(pieces_in)
    ).T
    pieces = list(pieces_of(totals[:, :size].reshape(-1), early))
    head_sums = totals[:, size : size + 2 * lanes].reshape(2, ctx, 2, lanes)
    head_sums = jnp.transpose(jnp.sum(head_sums, axis=0), (1, 0, 2)).reshape(2, -1)[:, :width]
    ln1 = list(pieces_of(jnp.sum(totals[:, size + 2 * lanes :], axis=0), late))
    up_grad = after(up_sums, totals)[:, :half_cols].astype(F32).T
    down_grad = after(down_grad, totals).astype(F32)
    out_weight_grad = after(out_sums, totals).astype(F32)

    return (
        layer_out.reshape(layer_in.shape),
        input_grad.reshape(layer_in.shape),
        ln1[0],
        ln1[1],
        qkv_grad,
        head_sums,
        out_weight_grad,
        pieces[0],
        pieces[1],
        pieces[2],
        up_grad,
        pieces[4],
        down_grad,
        pieces[3],
    )


def layer(ctx, *arrays):
    return shards(ctx, *arrays)


def solution(mesh):
    placed = (
        P("dp", "ctx", None),
        P("dp", "ctx", None),
        P("dp", None),
        P(),
        P(),
        P(None, "dp"),
        P(),
        P(None, "dp"),
        P(),
        P(),
        P(),
        P(None, "dp"),
        P(),
        P(None, "dp"),
        P(),
    )
    return jax.shard_map(
        partial(layer, mesh.shape["ctx"]),
        mesh=mesh,
        in_specs=placed,
        out_specs=(
            P("dp", "ctx", None),
            P("dp", "ctx", None),
            P(),
            P(),
            P("dp", "ctx"),
            P(),
            P("ctx", "dp"),
            P(),
            P(),
            P(),
            P("dp", "ctx"),
            P(),
            P("ctx", "dp"),
            P(),
        ),
        check_vma=False,
    )
```

```python
from functools import partial
import math

import jax
import jax.numpy as jnp
from jax import lax
from jax.experimental import pallas as pl
from jax.experimental.pallas import tpu as pltpu
from jax.sharding import PartitionSpec as P

from jax.experimental.layout import Layout, with_layout_constraint

HEADS = 25


EPS = 1e-05
GELU_C = 0.7978845608028654
NEG_FILL = -1e30
BF16 = jnp.bfloat16
F32 = jnp.float32


def normalize(data):
    centre = jnp.mean(data, axis=0, keepdims=True)
    shifted = data - centre
    inverse = lax.rsqrt(jnp.mean(shifted * shifted, axis=0, keepdims=True) + EPS)
    return (shifted * inverse, inverse)


def norm_back(grad_hat, normed, inverse):
    first_mean = jnp.mean(grad_hat, axis=0, keepdims=True)
    second = jnp.mean(grad_hat * normed, axis=0, keepdims=True)
    return inverse * (grad_hat - first_mean - normed * second)


def gelu_parts(values):
    cubic_term = 0.044715 * values * values * values
    tangent = jnp.tanh(GELU_C * (values + cubic_term))
    output = 0.5 * values * (1.0 + tangent)
    gelu_slope = 0.5 * (1.0 + tangent) + 0.5 * values * (1.0 - tangent * tangent) * GELU_C * (
        1.0 + 3.0 * 0.044715 * values * values
    )
    return (output, gelu_slope)


def head_parts(value, head_width):
    heads = value.shape[1] // head_width
    if heads == 1:
        return [value]
    lane = lax.broadcasted_iota(jnp.int32, value.shape, 1) // head_width
    return [jnp.where(lane == h, value, jnp.zeros_like(value)) for h in range(heads)]


def by_head(columns, shape, head_width):
    if len(columns) == 1:
        return jnp.broadcast_to(columns[0], shape)
    lane = lax.broadcasted_iota(jnp.int32, shape, 1) // head_width
    result = jnp.broadcast_to(columns[-1], shape)
    for h in range(len(columns) - 2, -1, -1):
        result = jnp.where(lane == h, columns[h], result)
    return result


def dot(a, b, contract):
    return lax.dot_general(a, b, (contract, ((), ())), preferred_element_type=F32)


def each_query_block(length, block, visit):
    if length // block <= 4:
        for index in range(length // block):
            chunks = [(0, index * block, False)] if index else []
            visit(index * block, chunks + [(index * block, block, True)])
    else:

        def step(index, carry):
            visit(pl.multiple_of(index * block, block), [(0, length, True)])
            return carry

        lax.fori_loop(0, length // block, step, 0)


def visible_mask(first_row, rows, first_key, keys):
    row_ids = first_row + lax.broadcasted_iota(jnp.int32, (rows, keys), 0)
    key_ids = first_key + lax.broadcasted_iota(jnp.int32, (rows, keys), 1)
    return key_ids <= row_ids


def slot_rows(order, seq, source, half):
    return [pl.multiple_of(order[seq, 2 * source + part] * half, half) for part in range(2)]


def forward_kernel(
    half, block, head_width, score_scale, order, qkv, slot_out, natural, out_rows, log_rows
):
    sources = qkv.shape[0]
    kinds, seqs, length, lanes = natural.shape

    def place(source, carry):
        for kind in range(kinds):
            rows = qkv[source, kind].T
            for seq in range(seqs):
                for part, first in enumerate(slot_rows(order, seq, source, half)):
                    begin = (2 * seq + part) * half
                    natural[kind, seq, pl.ds(first, half), :] = rows[begin : begin + half, :]
        return carry

    lax.fori_loop(0, sources, place, 0)

    def visit(seq, first_row, chunks):
        rows = pl.ds(first_row, block)
        queries = natural[0, seq, rows, :] * jnp.asarray(score_scale, BF16)
        outputs = []
        logs = []
        for query in head_parts(queries, head_width):
            scores = []
            for first_key, keys, masked in chunks:
                part = dot(query, natural[1, seq, first_key : first_key + keys, :], ((1,), (1,)))
                if masked:
                    part = jnp.where(
                        visible_mask(first_row, block, first_key, keys), part, NEG_FILL
                    )
                scores.append(part)
            top = jnp.max(scores[0], axis=1, keepdims=True)
            for part in scores[1:]:
                top = jnp.maximum(top, jnp.max(part, axis=1, keepdims=True))
            total = jnp.zeros((block, 1), F32)
            summed = jnp.zeros((block, lanes), F32)
            for (first_key, keys, masked), part in zip(chunks, scores):
                weights = jnp.exp(part - top)
                total = total + jnp.sum(weights, axis=1, keepdims=True)
                coarse = weights.astype(BF16)
                fine = (weights - coarse.astype(F32)).astype(BF16)
                values = natural[2, seq, first_key : first_key + keys, :]
                summed = summed + dot(coarse, values, ((1,), (0,))) + dot(fine, values, ((1,), (0,)))
            outputs.append(summed / total)
            logs.append(top + jnp.log(total))
        result = outputs[0]
        if len(outputs) > 1:
            lane = lax.broadcasted_iota(jnp.int32, result.shape, 1) // head_width
            for h in range(1, len(outputs)):
                result = jnp.where(lane == h, outputs[h], result)
        out_rows[seq, rows, :] = result.astype(BF16)
        log_rows[seq, rows, :] = by_head(logs, result.shape, head_width)

    def one_sequence(seq, carry):
        each_query_block(length, block, partial(visit, seq))
        return carry

    lax.fori_loop(0, seqs, one_sequence, 0)

    def give(source, carry):
        rows = [
            out_rows[seq, pl.ds(first, half), :]
            for seq in range(seqs)
            for first in slot_rows(order, seq, source, half)
        ]
        slot_out[source] = jnp.concatenate(rows, axis=0).T
        return carry

    lax.fori_loop(0, sources, give, 0)


def backward_kernel(
    half,
    block,
    head_width,
    score_scale,
    order,
    natural,
    out_rows,
    log_rows,
    grad_slots,
    slot_out,
    grad_rows,
    grad_natural,
):
    sources = grad_slots.shape[0]
    kinds, seqs, length, lanes = natural.shape

    def place(source, carry):
        rows = grad_slots[source].T
        for seq in range(seqs):
            for part, first in enumerate(slot_rows(order, seq, source, half)):
                begin = (2 * seq + part) * half
                grad_rows[seq, pl.ds(first, half), :] = rows[begin : begin + half, :]
        return carry

    lax.fori_loop(0, sources, place, 0)
    grad_natural[1:] = jnp.zeros((kinds - 1, seqs, length, lanes), F32)

    def visit(seq, first_row, chunks):
        rows = pl.ds(first_row, block)
        queries = natural[0, seq, rows, :] * jnp.asarray(score_scale, BF16)
        grads = grad_rows[seq, rows, :]
        products = grads.astype(F32) * out_rows[seq, rows, :].astype(F32)
        logs = log_rows[seq, rows, :]
        query_sum = jnp.zeros(products.shape, F32)
        parts = zip(
            head_parts(queries, head_width),
            head_parts(grads, head_width),
            head_parts(products, head_width),
        )
        for h, (query, grad, product) in enumerate(parts):
            delta = jnp.sum(product, axis=1, keepdims=True)
            log_total = logs[:, h * head_width : h * head_width + 1]
            for first_key, keys, masked in chunks:
                span = slice(first_key, first_key + keys)
                key_block = natural[1, seq, span, :]
                scores = dot(query, key_block, ((1,), (1,)))
                probs = jnp.exp(scores - log_total)
                if masked:
                    probs = jnp.where(
                        visible_mask(first_row, block, first_key, keys), probs, 0.0
                    )
                grad_probs = dot(grad, natural[2, seq, span, :], ((1,), (1,)))
                grad_scores = (probs * (grad_probs - delta)).astype(BF16)
                grad_natural[2, seq, span, :] += dot(probs.astype(BF16), grad, ((0,), (0,)))
                grad_natural[1, seq, span, :] += dot(grad_scores, query, ((0,), (0,)))
                query_sum = query_sum + dot(
                    grad_scores, head_parts(key_block, head_width)[h], ((1,), (0,))
                )
        grad_natural[0, seq, rows, :] = query_sum * score_scale

    def one_sequence(seq, carry):
        each_query_block(length, block, partial(visit, seq))
        return carry

    lax.fori_loop(0, seqs, one_sequence, 0)

    def give(source, carry):
        for kind in range(kinds):
            rows = [
                grad_natural[kind, seq, pl.ds(first, half), :]
                for seq in range(seqs)
                for first in slot_rows(order, seq, source, half)
            ]
            slot_out[source, kind] = jnp.concatenate(rows, axis=0).astype(BF16).T
        return carry

    lax.fori_loop(0, sources, give, 0)


def in_vmem(count):
    return [pl.BlockSpec(memory_space=pltpu.VMEM)] * count


def attend_forward(qkv, order, head_width, score_scale):
    sources, kinds, lanes, tokens = qkv.shape
    seqs = order.shape[0]
    length = sources * tokens // seqs
    block = math.gcd(length, 256)
    return pl.pallas_call(
        partial(forward_kernel, tokens // seqs // 2, block, head_width, score_scale),
        in_specs=[pl.BlockSpec(memory_space=pltpu.SMEM)] + in_vmem(1),
        out_specs=in_vmem(4),
        out_shape=[
            jax.ShapeDtypeStruct((sources, lanes, tokens), BF16),
            jax.ShapeDtypeStruct((kinds, seqs, length, lanes), BF16),
            jax.ShapeDtypeStruct((seqs, length, lanes), BF16),
            jax.ShapeDtypeStruct((seqs, length, lanes), F32),
        ],
        name="attf",
    )(order, qkv)


def attend_backward(natural, out_rows, log_rows, grad_slots, order, head_width, score_scale):
    sources, lanes, tokens = grad_slots.shape
    kinds, seqs, length, lanes = natural.shape
    block = math.gcd(length, 256)
    return pl.pallas_call(
        partial(backward_kernel, tokens // seqs // 2, block, head_width, score_scale),
        in_specs=[pl.BlockSpec(memory_space=pltpu.SMEM)] + in_vmem(4),
        out_specs=in_vmem(1)[0],
        scratch_shapes=[
            pltpu.VMEM((seqs, length, lanes), BF16),
            pltpu.VMEM((kinds, seqs, length, lanes), F32),
        ],
        out_shape=jax.ShapeDtypeStruct((sources, kinds, lanes, tokens), BF16),
        name="attb",
    )(order, natural, out_rows, log_rows, grad_slots)


def product_kernel(flip, kept, got, own, side, core, *parts):
    units, tokens = kept.shape[0], own.shape[1]
    halves = 2
    width = parts[0].shape[-1]
    block = own.shape[0] // halves
    pairs = (
        (kept, 0, own, 0),
        (kept, tokens, core, 0),
        (got, 0, side, 0),
        (got, tokens, core, tokens),
    )
    step = units // 2

    def one_half(half, carry):
        for first in range(0, units, step):
            total = jnp.zeros((step, block), F32)
            for left, left_at, right, right_at in pairs:
                a = left[first : first + step, left_at : left_at + tokens]
                rows = pl.ds(pl.multiple_of((half ^ flip[0]) * block, 16), block)
                b = right[rows, right_at : right_at + tokens]
                total = total + dot(a, b, ((1,), (1,)))
            total = total.astype(BF16)
            if width > block:
                total = jnp.concatenate([total, jnp.zeros((step, width - block), BF16)], axis=1)
            if len(parts) == 1:
                parts[0][half, first : first + step] = total
            else:
                for index, part in enumerate(parts):

                    @pl.when(half == index)
                    def _(part=part):
                        part[first : first + step] = total

        return carry

    lax.fori_loop(0, halves, one_half, 0)


def tokens_product(units, rows, flip, apart):
    kept, got = units
    own, side, core = rows
    width = own.shape[0] // 2
    whole = (2, kept.shape[0], width + -width % 128)
    return pl.pallas_call(
        product_kernel,
        in_specs=[pl.BlockSpec(memory_space=pltpu.SMEM)] + in_vmem(5),
        out_specs=in_vmem(2) if apart else in_vmem(1)[0],
        out_shape=[jax.ShapeDtypeStruct(whole[1:], BF16)] * 2
        if apart
        else jax.ShapeDtypeStruct(whole, BF16),
        name="prod",
    )(jnp.full((1,), flip, jnp.int32), kept, got, own, side, core)


def rounds_of(edges):
    at_source, at_target = {}, {}
    for source, target, item in edges:
        sends, gets = at_source.setdefault(source, {}), at_target.setdefault(target, {})
        first = next(r for r in range(len(edges)) if r not in sends)
        last = next(r for r in range(len(edges)) if r not in gets)
        if first != last:
            path, node, side, look = [], target, at_target, first
            while look in side.setdefault(node, {}):
                edge = side[node][look]
                path.append((edge, look))
                node = edge[0] if side is at_target else edge[1]
                side = at_source if side is at_target else at_target
                look = first + last - look
            for edge, was in path:
                del at_source[edge[0]][was], at_target[edge[1]][was]
            for edge, was in path:
                now = first + last - was
                at_source[edge[0]][now] = at_target[edge[1]][now] = edge
        sends[first] = gets[first] = (source, target, item)
    count = 1 + max(r for sends in at_source.values() for r in sends)
    return [[sends[r] for sends in at_source.values() if r in sends] for r in range(count)]


def to_heads(data, devices, lanes):
    width, tokens = data.shape
    return jnp.pad(data, ((0, devices * lanes - width), (0, 0))).reshape(devices, lanes, tokens)


def from_heads(blocks, width):
    devices, lanes, tokens = blocks.shape
    return blocks.reshape(devices * lanes, tokens)[:width]


def shards(
    ctx,
    layer_in,
    out_grad,
    block_order,
    ln1_gain,
    ln1_bias,
    w_qkv,
    qv_bias,
    w_out,
    out_bias,
    ln2_gain,
    ln2_bias,
    w_up,
    up_bias,
    w_down,
    down_bias,
):
    seqs, tok_rows, width = layer_in.shape
    tokens = seqs * tok_rows
    head_width = width // HEADS
    score_scale = 1.0 / math.sqrt(head_width)
    lanes = -(-HEADS // ctx) * head_width
    half_units = w_up.shape[1]
    half_cols = w_out.shape[1]
    half_proj = w_qkv.shape[1]
    planes = ctx // 4
    my_dp = lax.axis_index("dp")
    my_ctx = lax.axis_index("ctx")
    my_core = my_ctx % 2
    my_side = (my_ctx // 2) % 2
    core_swap = [(i, i ^ 1) for i in range(ctx)]
    side_swap = [(i, i ^ 2) for i in range(ctx)]
    lines = [[q + 4 * z for z in range(planes)] for q in range(4)]

    def across(x):
        return lax.ppermute(x, "dp", [(0, 1), (1, 0)])

    def to_core(x):
        return lax.ppermute(x, "ctx", core_swap)

    def to_side(x):
        return lax.ppermute(x, "ctx", side_swap)

    def exchange(x):
        return lax.all_to_all(x, "ctx", 0, 0, tiled=True)

    def after(x, *earlier):
        return lax.optimization_barrier((x,) + earlier)[0]

    def pick(x, index, axis, count=2):
        size = x.shape[axis] // count
        return lax.dynamic_slice_in_dim(x, index * size, size, axis)

    def split(x, index, axis):
        return pick(x, index, axis), pick(x, 1 - index, axis)

    def joined(index, mine, other, axis=0):
        return jnp.where(
            index == 0,
            jnp.concatenate([mine, other], axis=axis),
            jnp.concatenate([other, mine], axis=axis),
        )

    def dot32(a, b, spec):
        return jnp.einsum(spec, a, b, preferred_element_type=F32)

    column = lambda vector: vector[:, None]

    own_in = layer_in.reshape(tokens, width).T
    own_out_grad = out_grad.reshape(tokens, width).T
    other_in = across(own_in)
    stream = own_in.astype(F32)
    normed_one, inverse_one = normalize(stream)
    gain_one, bias_one = column(ln1_gain), column(ln1_bias)
    hidden_one = (normed_one * gain_one + bias_one).astype(BF16)
    hidden_one_other = (normalize(other_in.astype(F32))[0] * gain_one + bias_one).astype(BF16)
    hidden_one_other = lax.optimization_barrier(hidden_one_other)
    proj_bias = jnp.concatenate([qv_bias[0], jnp.zeros_like(qv_bias[0]), qv_bias[1]])
    proj_bias = column(pick(proj_bias, my_dp, 0))
    proj_other = (dot32(w_qkv, hidden_one_other, "de,dt->et") + proj_bias).astype(BF16)
    proj_got = across(proj_other)
    proj_own = (dot32(w_qkv, hidden_one, "de,dt->et") + proj_bias).astype(BF16)
    proj_own = lax.optimization_barrier(proj_own)
    low = jnp.where(my_dp == 0, proj_own, proj_got)
    high = jnp.where(my_dp == 0, proj_got, proj_own)
    queries = low[:width]
    keys = jnp.concatenate([low[width:], high[: 2 * width - half_proj]], axis=0)
    values = high[2 * width - half_proj :]
    send = jnp.stack([to_heads(x, ctx, lanes) for x in (queries, keys, values)], axis=1)
    qkv_heads = exchange(send)

    out_mine = across(after(pick(w_out, my_core, 0), proj_got))
    other_out_grad = across(after(own_out_grad, proj_got))
    down_rows = pick(w_down, my_dp, 0)
    down_send = pick(pick(w_down, 1 - my_dp, 0), my_core, 1)
    down_mine = across(after(down_send, proj_got))
    out_rest = to_core(after(out_mine, qkv_heads))

    hidden_one_all = lax.all_gather(after(hidden_one.T, qkv_heads), "ctx", axis=0, tiled=True)

    attended_slots, natural, out_rows, log_rows = attend_forward(
        qkv_heads, block_order, head_width, score_scale
    )
    attended = from_heads(exchange(attended_slots), width)
    down_rest = to_core(after(down_mine, attended))

    attended_mine, attended_rest = split(attended, my_core, 0)
    mixed = joined(
        my_dp,
        dot32(w_out, attended, "ab,at->bt"),
        dot32(out_mine, attended_mine, "ab,at->bt") + dot32(out_rest, attended_rest, "ab,at->bt"),
    )
    residual = stream + mixed + column(out_bias)
    normed_two, inverse_two = normalize(residual)
    gain_two = column(ln2_gain)
    hidden_two = (normed_two * gain_two + column(ln2_bias)).astype(BF16)
    hidden_two_pair = jnp.concatenate([hidden_two, across(hidden_two)], axis=1)

    out_grad_pair = after(
        jnp.concatenate([own_out_grad, after(other_out_grad, attended)], axis=1), hidden_two
    )
    out_grad_own, out_grad_rest = split(out_grad_pair, my_dp, 0)
    rest_mine, rest_rest = split(out_grad_rest, my_core, 0)
    grad_active = (
        dot32(down_rows, out_grad_own, "fd,dt->ft")
        + dot32(down_mine, rest_mine, "fd,dt->ft")
        + dot32(down_rest, rest_rest, "fd,dt->ft")
    )
    pre_act = dot32(w_up, hidden_two_pair, "df,dt->ft") + column(pick(up_bias, my_dp, 0))
    activated_wide, gelu_slope = gelu_parts(pre_act)
    activated = with_layout_constraint(activated_wide.astype(BF16), Layout((0, 1)))
    grad_pre = with_layout_constraint((grad_active * gelu_slope).astype(BF16), Layout((0, 1)))
    grad_two = dot32(grad_pre, w_up, "ft,df->dt")
    two_send = grad_two[:, tokens:].astype(BF16)
    grad_two_got = across(two_send)
    grad_hidden_two = grad_two[:, :tokens] + grad_two_got.astype(F32)

    grad_out = own_out_grad.astype(F32)
    grad_residual = grad_out + norm_back(grad_hidden_two * gain_two, normed_two, inverse_two)
    grad_mixed = grad_residual.astype(BF16)
    mixed_own, mixed_other = split(grad_mixed, my_dp, 0)
    grad_attended = (
        dot32(w_out, mixed_own, "ab,bt->at")
        + joined(
            my_core,
            dot32(out_mine, mixed_other, "ab,bt->at"),
            dot32(out_rest, mixed_other, "ab,bt->at"),
        )
    ).astype(BF16)
    middle_sums = [
        jnp.sum(grad_mixed.astype(F32), axis=1),
        jnp.sum(grad_hidden_two * normed_two, axis=1),
        jnp.sum(grad_hidden_two, axis=1),
        jnp.sum(grad_out, axis=1),
        jnp.sum(grad_pre.astype(F32), axis=1),
    ]
    grad_send, *middle_sums = lax.optimization_barrier(
        [to_heads(grad_attended, ctx, lanes)] + middle_sums
    )
    grad_slots = exchange(grad_send)

    def plane_rows(data, later):
        side = after(to_side(data), *later)
        return data, side, to_core(jnp.concatenate([data, side], axis=-1))

    def plane_units(units, later):
        size = units.shape[0] // (planes // 2 * 4)
        grid = units.reshape(planes // 2, 2, 2, size, units.shape[1])
        kept, sent = split(grid, my_core, 2)
        both = jnp.concatenate([kept, after(to_core(sent), *later)], axis=-1)
        kept, sent = split(both, my_side, 1)
        return kept, to_side(sent)

    def flat(units):
        return units.reshape(-1, units.shape[-1])

    def line_sum(parts):
        return lax.psum_scatter(
            parts, "ctx", scatter_dimension=0, axis_index_groups=lines, tiled=False
        )

    active_kept, active_got = plane_units(activated, (grad_two,))
    pre_kept, pre_got = plane_units(grad_pre, (two_send,))
    out_grad_early = jnp.concatenate([own_out_grad, after(other_out_grad, qkv_heads)], axis=1)
    out_grad_all = plane_rows(out_grad_early, (two_send,))

    units = (flat(active_kept), flat(after(active_got, two_send)))
    down_parts = tokens_product(units, out_grad_all, 0, False)
    down_parts = down_parts.reshape(planes, -1, down_parts.shape[2])
    hidden_two_all = plane_rows(hidden_two_pair, (two_send,))
    units = (flat(pre_kept), flat(after(pre_got, down_parts)))
    up_kept, up_sent = tokens_product(units, hidden_two_all, my_dp, True)
    up_got = across(up_sent)

    line_ready = after(down_parts, hidden_one_all)
    down_sums = line_sum(line_ready)[:, :half_cols]
    owner = [
        (d * ctx + (e * planes // 2 + z) * 4 + q, e * ctx + (d * planes // 2 + z) * 4 + q)
        for d in range(2)
        for e in range(2)
        for z in range(planes // 2)
        for q in range(4)
    ]

    proj_slots = attend_backward(
        natural,
        out_rows,
        log_rows,
        after(grad_slots, line_ready),
        block_order,
        head_width,
        score_scale,
    )
    proj_back = exchange(proj_slots)
    grad_proj = jnp.concatenate(
        [from_heads(proj_back[:, kind], width) for kind in range(3)], axis=0
    )
    down_grad = lax.ppermute(after(down_sums, proj_slots), ("dp", "ctx"), owner)

    unit_block = 2 * half_units // ctx
    up_parts = joined(my_dp, up_kept, after(up_got, proj_slots))
    up_parts = up_parts.reshape(planes, unit_block, -1)
    up_sums = line_sum(up_parts)
    proj_mine, proj_rest = split(grad_proj, my_dp, 0)
    proj_pair = jnp.concatenate([proj_mine, across(proj_rest)], axis=1)
    grad_one = dot32(w_qkv, proj_pair, "de,et->dt")
    one_send = grad_one[:, tokens:].astype(BF16)
    grad_one_got = across(one_send)
    grad_hidden_one = grad_one[:, :tokens] + grad_one_got.astype(F32)
    input_grad = grad_residual + norm_back(grad_hidden_one * gain_one, normed_one, inverse_one)
    input_grad = input_grad.astype(BF16).T

    attended_late = after(attended, hidden_two)
    attended_got = after(across(attended_late), proj_back)
    attended_pair = jnp.concatenate([attended_late, attended_got], axis=1)
    size = width // ctx
    grid = attended_pair.reshape(planes, 2, 2, size, 2 * tokens)
    kept, sent = split(grid, my_core, 2)
    both = jnp.concatenate([kept, to_core(sent)], axis=-1)
    kept, sent = split(both, my_side, 1)
    out_units = (kept, after(to_side(sent), proj_slots))
    mixed_pair = jnp.concatenate([mixed_own, after(across(mixed_other), proj_back)], axis=1)
    mixed_all = plane_rows(mixed_pair, (one_send,))
    out_part = 0.0
    step = 2 * tokens
    kept, got = [flat(units) for units in out_units]
    for units, at, rows in ((kept, 0, 0), (kept, 1, 2), (got, 0, 1), (got, 1, 2)):
        begin = step if rows == 2 and units is got else 0
        rows = mixed_all[rows][:, begin : begin + step]
        out_part += dot32(units[:, at * step : (at + 1) * step], rows, "ct,dt->cd")
    out_part = out_part.astype(BF16)
    out_part = out_part.reshape(planes, size, half_cols)
    my_plane = my_ctx // 4
    if planes > 4:
        out_part = jnp.pad(out_part, ((0, 0), (0, -size % 8), (0, -half_cols % 128)))
        out_sums = [line_sum(out_part)[:size, :half_cols]]
    else:
        out_sums = [lax.dynamic_index_in_dim(out_part, my_plane, 0, keepdims=False)]
        for step in range(1, planes):
            target = (my_plane + step) % planes
            piece = lax.dynamic_index_in_dim(out_part, target, 0, keepdims=False)
            pairs = [(k, (k + 4 * step) % ctx) for k in range(ctx)]
            out_sums.append(lax.ppermute(piece, "ctx", pairs))

    qkv_part = dot32(
        proj_slots, hidden_one_all.reshape(ctx, tokens, width), "sklt,std->dkl"
    )
    qkv_kept, qkv_send = split(qkv_part, my_dp, 0)
    qkv_send = qkv_send.astype(BF16)
    qkv_got = across(qkv_send)
    qkv_sums = (qkv_kept + qkv_got.astype(F32)).astype(BF16)
    block = 2 * half_proj // ctx
    edges = []
    for source in range(ctx):
        for kind in range(3):
            first = kind * width + source * lanes
            last = min(first + lanes, (kind + 1) * width)
            if first < last:
                for target in range(first // block, (last - 1) // block + 1):
                    edges.append((source, target, kind))
    rounds = rounds_of(edges)
    kinds = [[0] * ctx for _ in rounds]
    offsets = [[-lanes] * ctx for _ in rounds]
    for number, edges_now in enumerate(rounds):
        for source, target, kind in edges_now:
            kinds[number][source] = kind
            offsets[number][target] = kind * width + source * lanes - target * block
    mine = jnp.arange(ctx, dtype=jnp.int32)[None, :] == my_ctx
    kinds = jnp.sum(jnp.where(mine, jnp.asarray(kinds, jnp.int32), 0), axis=1)
    offsets = jnp.sum(jnp.where(mine, jnp.asarray(offsets, jnp.int32), 0), axis=1)
    place = offsets[:, None, None] + jnp.arange(lanes, dtype=jnp.int32)[None, :, None]
    targets = jnp.arange(block, dtype=jnp.int32)[None, None, :]
    chosen = (targets == place).astype(BF16)
    pieces = [
        jnp.where(kind == 0, qkv_sums[:, 0], jnp.where(kind == 1, qkv_sums[:, 1], qkv_sums[:, 2]))
        for kind in kinds
    ]
    received = []
    for number, edges_now in enumerate(rounds):
        piece = lax.ppermute(pieces[number], "ctx", [edge[:2] for edge in edges_now])
        received.append(piece)

    activated_late = after(activated, grad_one_got)
    down_sum = joined(
        my_dp,
        dot32(activated_late, down_rows, "ft,fd->dt"),
        joined(
            my_core,
            dot32(activated_late, down_mine, "ft,fd->dt"),
            dot32(activated_late, down_rest, "ft,fd->dt"),
        ),
    )
    down_got = across(down_sum[:, tokens:].astype(BF16))
    layer_out = residual + (down_sum[:, :tokens] + down_got.astype(F32)) + column(down_bias)
    layer_out = layer_out.astype(BF16).T

    def at_dp(vector):
        none = jnp.zeros_like(vector)
        return joined(my_dp, vector, none)

    devices = 2 * ctx

    def everywhere(packed):
        return lax.all_to_all(packed, ("dp", "ctx"), 0, 0, tiled=True)

    def pieces_of(totals, items):
        first = 0
        for item in items:
            yield totals[first : first + item.shape[0]]
            first += item.shape[0]

    early = middle_sums[:4] + [at_dp(middle_sums[4])]
    packed = after(jnp.concatenate(early), grad_slots)
    size = -(-packed.shape[0] // (devices * 128)) * 128
    packed = jnp.pad(packed, (0, devices * size - packed.shape[0]))
    mine = everywhere(packed.reshape(devices, size // 128, 128))
    mine = jnp.sum(mine, axis=0).reshape(-1)
    head_sums = jnp.sum(proj_slots.astype(F32), axis=(0, 3))
    late = [jnp.sum(grad_hidden_one * normed_one, axis=1), jnp.sum(grad_hidden_one, axis=1)]
    packed = jnp.concatenate([mine, head_sums[0], head_sums[2]] + late)
    packed = jnp.pad(packed, (0, -packed.shape[0] % 128)).reshape(1, -1, 128)
    packed = jnp.broadcast_to(packed, (devices,) + packed.shape[1:])
    totals = everywhere(packed).reshape(devices, -1)
    pieces_in = [after(piece, packed) for piece in received]
    qkv_grad = sum(
        dot32(piece, chosen[i], "dr,rc->dc") for i, piece in enumerate(pieces_in)
    )
    pieces = list(pieces_of(totals[:, :size].reshape(-1), early))
    head_sums = totals[:, size : size + 2 * lanes].reshape(2, ctx, 2, lanes)
    head_sums = jnp.transpose(jnp.sum(head_sums, axis=0), (1, 0, 2)).reshape(2, -1)[:, :width]
    ln1 = list(pieces_of(jnp.sum(totals[:, size + 2 * lanes :], axis=0), late))
    up_grad = after(up_sums, totals)[:, :half_cols].astype(F32).T
    down_grad = after(down_grad, totals).astype(F32)
    out_weight_grad = sum(after(piece, totals).astype(F32) for piece in out_sums)

    return (
        layer_out.reshape(layer_in.shape),
        input_grad.reshape(layer_in.shape),
        ln1[0],
        ln1[1],
        qkv_grad,
        head_sums,
        out_weight_grad,
        pieces[0],
        pieces[1],
        pieces[2],
        up_grad,
        pieces[4],
        down_grad,
        pieces[3],
    )


def layer(ctx, *arrays):
    return shards(ctx, *arrays)


def solution(mesh):
    placed = (
        P("dp", "ctx", None),
        P("dp", "ctx", None),
        P("dp", None),
        P(),
        P(),
        P(None, "dp"),
        P(),
        P(None, "dp"),
        P(),
        P(),
        P(),
        P(None, "dp"),
        P(),
        P(None, "dp"),
        P(),
    )
    return jax.shard_map(
        partial(layer, mesh.shape["ctx"]),
        mesh=mesh,
        in_specs=placed,
        out_specs=(
            P("dp", "ctx", None),
            P("dp", "ctx", None),
            P(),
            P(),
            P("dp", "ctx"),
            P(),
            P("ctx", "dp"),
            P(),
            P(),
            P(),
            P("dp", "ctx"),
            P(),
            P("ctx", "dp"),
            P(),
        ),
        check_vma=False,
    )
```
